32 devices in a mesh: groups: 2 (over y), ctx: 4 (over z), heads: 2 (over x), rep: 2 (over core).
Axes of the slice: x: 2, y: 2, z: 4, core: 2. Of those that a mesh axis runs over, the one named last changes fastest.
Arguments:
- queries: bfloat16 [24576, 32, 128], P(('groups', 'ctx'), ('heads', 'rep')), parts along dimension 0, may hold values from -14 to 14
- keys: bfloat16 [24576, 8, 128], P(('groups', 'ctx'), 'heads'), parts along dimension 0, may hold values from -14 to 14
- values: bfloat16 [24576, 8, 128], P(('groups', 'ctx'), 'heads'), parts along dimension 0, may hold values from -6 to 6
- chosen: int32 [8, 192, 8], P('heads', ('groups', 'ctx')), parts along dimension 1, may hold values from 0 to 95, as said below
Outputs:
- attended: bfloat16 [24576, 32, 128], P(('groups', 'ctx'), ('heads', 'rep')), parts along dimension 0
The draws below stay inside these ranges and needn't reach their ends.
There are 2 independent parts, one for each index of `groups`. The reference program is written for one: setup_inputs(seed, part) draws one part's arguments, and reference() takes and returns one part's arrays. A program takes and returns all parts, laid end to end along the dimension named above; each array names one. Nothing has to cross between parts.
Inputs may be any that keep to these rules, and one draw needn't show every extreme that they name: chosen[h, b, 0] = b. The other entries of a list are at most b and differ from each other, except that b itself may be repeated. For one key-value head, the 24 query blocks of one sequence shard list at most 2 distinct blocks of any other shard.
All inputs are finite; a program needn't handle non-finite values.
Results may differ from the reference program's by a relative error of at most 0.0046.
Values may be sent and summed in bfloat16 or wider, within the bound.
A program may use at most 128 MiB of HBM per device.

```python
import jax
import jax.numpy as jnp
from jax import lax

QUERY_HEADS = 32
KEY_VALUE_HEADS = 8
HEAD_SIZE = 128
TOPK = 8
REMOTE_BLOCK_MAX = 2
QB_DEV = 24
CTX_SHARDS = 4
SEQUENCE_TOKENS = 12288


def pair_draw(key):
    pair_key = jax.random.fold_in(key, 7)
    key_seed_first, key_two = jax.random.split(pair_key, 2)
    key_pattern = jnp.clip(jax.random.normal(key_seed_first, (SEQUENCE_TOKENS, KEY_VALUE_HEADS, HEAD_SIZE), jnp.float32), -4.0, 4.0)
    query_field = jnp.clip(jax.random.normal(key_two, (SEQUENCE_TOKENS, QUERY_HEADS, HEAD_SIZE), jnp.float32), -4.0, 4.0)
    return (query_field, key_pattern)


def draw_queries(key, part):
    return pair_draw(key)[0].astype(jnp.bfloat16)


def draw_keys(key, part):
    return pair_draw(key)[1].astype(jnp.bfloat16)


def draw_chosen(key, part):
    shard_count = CTX_SHARDS
    blocks_per_shard = QB_DEV
    block_count = shard_count * blocks_per_shard
    leading_key, following_key = jax.random.split(jax.random.fold_in(key, 11))
    unscaled_scores = jax.random.randint(leading_key, (KEY_VALUE_HEADS, shard_count, shard_count, blocks_per_shard), 0, 1 << 20) * blocks_per_shard + jnp.arange(blocks_per_shard, dtype=jnp.int32)
    unused_score, selected_resident = lax.top_k(unscaled_scores, REMOTE_BLOCK_MAX)
    source_offset = (jnp.arange(shard_count, dtype=jnp.int32) * blocks_per_shard)[None, None, :, None]
    remote_blocks = (source_offset + selected_resident).reshape(KEY_VALUE_HEADS, shard_count, shard_count * REMOTE_BLOCK_MAX)
    block_numbers = jnp.arange(block_count, dtype=jnp.int32)
    device_of = block_numbers // blocks_per_shard
    within = block_numbers % blocks_per_shard
    remote_rows = jnp.repeat(remote_blocks, blocks_per_shard, axis=1)
    resident_rows = device_of[:, None] * blocks_per_shard + jnp.arange(blocks_per_shard, dtype=jnp.int32)[None, :]
    resident_rows = jnp.broadcast_to(resident_rows[None], (KEY_VALUE_HEADS, block_count, blocks_per_shard))
    candidates = jnp.concatenate([remote_rows, resident_rows], axis=-1)
    full_width = shard_count * REMOTE_BLOCK_MAX + blocks_per_shard
    slot_table = jnp.arange(full_width, dtype=jnp.int32)
    remote_valid = jnp.arange(shard_count * REMOTE_BLOCK_MAX, dtype=jnp.int32)[None, :] // REMOTE_BLOCK_MAX < device_of[:, None]
    local_valid = jnp.arange(blocks_per_shard, dtype=jnp.int32)[None, :] < within[:, None]
    valid = jnp.concatenate([remote_valid, local_valid], axis=-1)[None]
    full_scores = jax.random.randint(following_key, (KEY_VALUE_HEADS, block_count, full_width), 0, 1 << 20) * full_width + slot_table
    live_count = jnp.maximum(device_of * REMOTE_BLOCK_MAX, 1)[:, None]
    forced = jnp.zeros((block_count, full_width), dtype=bool)
    for turn in range(3):
        forced = forced | (slot_table[None, :] == (within[:, None] + turn * blocks_per_shard) % live_count)
    forced = forced & (device_of[:, None] >= 1)
    full_scores = jnp.where(forced[None], (1 << 20) * full_width + full_width + slot_table, full_scores)
    full_scores = jnp.where(valid, full_scores, -1 - slot_table)
    best_score, best_index = lax.top_k(full_scores, TOPK - 1)
    picked = jnp.take_along_axis(candidates, best_index, axis=-1)
    picked = jnp.where(best_score >= 0, picked, block_numbers[None, :, None])
    own_device = jnp.broadcast_to(block_numbers[None, :, None], (KEY_VALUE_HEADS, block_count, 1))
    return jnp.concatenate([own_device, picked], axis=-1).astype(jnp.int32)


def steps_of(own_key, extent, cuts, least, largest):
    gain = 1.0
    for position, parts in cuts:
        draws = jax.random.uniform(jax.random.fold_in(jax.random.fold_in(own_key, 6), position), (parts,), jnp.float32, least / len(cuts), largest / len(cuts))
        gain = gain * jnp.repeat(jnp.exp(draws), extent[position] // parts).reshape((-1,) + (1,) * (len(extent) - 1 - position))
    return gain


def centred(own_key, shape, deviation, reach, shards=(), kind=jnp.bfloat16):
    factor_of = steps_of(own_key, shape, shards, -0.22, 0.18) if shards else 1.0
    drawn = jax.random.normal(own_key, shape, jnp.float32) * deviation * factor_of
    return jnp.minimum(jnp.maximum(drawn, -reach), reach).astype(kind)


def setup_inputs(seed: int = 0, part: int = 0) -> dict:
    key_of = jax.random.split(jax.random.key(seed), 5)
    part_keys = jax.random.split(jax.random.fold_in(key_of[4], part), 5)
    return {
        "queries": draw_queries(jax.random.fold_in(jax.random.fold_in(key_of[4], part), 71), part),
        "keys": draw_keys(jax.random.fold_in(jax.random.fold_in(key_of[4], part), 71), part),
        "values": centred(part_keys[2], (SEQUENCE_TOKENS, KEY_VALUE_HEADS, HEAD_SIZE), 1.0, 6.0, ((0, 4), (1, 2))),
        "chosen": draw_chosen(jax.random.fold_in(jax.random.fold_in(key_of[4], part), 71), part),
    }


def attend(query_part, key_part, value_part, chosen_part):
    block_len = query_part.shape[1]
    head_dim = query_part.shape[-1]
    picks = chosen_part.shape[-1]
    scores = jnp.einsum("gqeah,egkh->egaqk", query_part.astype(jnp.float32), key_part.astype(jnp.float32)) * (head_dim ** -0.5)
    earlier = chosen_part[..., :, None] == chosen_part[..., None, :]
    before_slot = jnp.arange(picks)[:, None] > jnp.arange(picks)[None, :]
    repeated = jnp.any(earlier & before_slot[None, None], axis=-1)
    slot_open = jnp.repeat(jnp.logical_not(repeated), block_len, axis=-1)
    key_slot = jnp.arange(picks * block_len) // block_len
    key_place = jnp.arange(picks * block_len) % block_len
    query_place = jnp.arange(block_len)
    causal = (key_slot[None, :] > 0) | (key_place[None, :] <= query_place[:, None])
    visible = slot_open[:, :, None, None, :] & causal[None, None, None]
    highest = jnp.max(jnp.where(visible, scores, -jnp.inf), axis=-1, keepdims=True)
    weights = jnp.where(visible, jnp.exp(scores - highest), jnp.float32(0.0))
    totals = jnp.sum(weights, axis=-1)
    probabilities = lax.optimization_barrier(weights.astype(jnp.bfloat16)).astype(jnp.float32)
    attended = jnp.einsum("egaqk,egkh->gqeah", probabilities, value_part.astype(jnp.float32))
    scaled = attended / jnp.transpose(totals, (1, 3, 0, 2))[..., None]
    return scaled.astype(jnp.bfloat16)


def reference(queries, keys, values, chosen):
    tokens_all, query_heads, head_dim = queries.shape
    kv_heads = keys.shape[1]
    blocks = chosen.shape[1]
    picks = chosen.shape[2]
    block_len = tokens_all // blocks
    heads_per_group = query_heads // kv_heads
    group_size = 4

    def one_head(head_number):
        query_head = lax.dynamic_slice_in_dim(queries, head_number * heads_per_group, heads_per_group, 1)
        key_blocks = lax.dynamic_slice_in_dim(keys, head_number, 1, 1).reshape(blocks, block_len, head_dim)
        value_blocks = lax.dynamic_slice_in_dim(values, head_number, 1, 1).reshape(blocks, block_len, head_dim)
        chosen_head = lax.dynamic_index_in_dim(chosen, head_number, 0, keepdims=False)
        query_groups = query_head.reshape(blocks // group_size, group_size, block_len, 1, heads_per_group, head_dim)
        chosen_groups = chosen_head.reshape(blocks // group_size, group_size, picks)

        def block_group(operands):
            query_part, chosen_part = operands
            key_part = key_blocks[chosen_part].reshape(1, group_size, picks * block_len, head_dim)
            value_part = value_blocks[chosen_part].reshape(1, group_size, picks * block_len, head_dim)
            return attend(query_part, key_part, value_part, chosen_part[None])

        result = lax.map(block_group, (query_groups, chosen_groups))
        return result.reshape(tokens_all, heads_per_group, head_dim)

    stacked = lax.map(one_head, jnp.arange(kv_heads, dtype=jnp.int32))
    return jnp.transpose(stacked, (1, 0, 2, 3)).reshape(tokens_all, query_heads, head_dim)
```

```python
import functools
import math

import jax
import jax.numpy as jnp
from jax import lax
from jax.experimental import pallas as pl
from jax.experimental.pallas import tpu as pltpu
from jax.sharding import PartitionSpec as P

QUERY_HEADS = 32
KEY_VALUE_HEADS = 8
REMOTE_BLOCK_MAX = 2
NEGATIVE = -1e30
BIG = 1 << 30
PLAN_ROWS = 16
OPEN, CAUSAL, CLOSED = 0, 1, 2
MESH = pl.DeviceIdType.MESH


def fill_masks(hot, aux):
    width, block_len = hot.shape
    row = lax.div(lax.broadcasted_iota(jnp.int32, (width, block_len), 0), width // block_len)
    lane = lax.broadcasted_iota(jnp.int32, (width, block_len), 1)
    hot[...] = jnp.where(row == lane, 1.0, 0.0).astype(jnp.bfloat16)
    key = lax.broadcasted_iota(jnp.int32, (block_len, block_len), 0)
    query = lax.broadcasted_iota(jnp.int32, (block_len, block_len), 1)
    aux[OPEN] = jnp.zeros((block_len, block_len), jnp.bfloat16)
    aux[CAUSAL] = jnp.where(key <= query, 0.0, NEGATIVE).astype(jnp.bfloat16)
    aux[CLOSED] = jnp.full((block_len, block_len), NEGATIVE, jnp.bfloat16)


def score(q, keys, masks, hot, aux, kt_ref, s_ref, t_ref):
    block_len = kt_ref.shape[1]
    width = q.shape[0]
    qa = jnp.concatenate([q, hot[...]], axis=1)
    ka = jnp.concatenate(
        [jnp.concatenate([kt_ref[k], aux[a]], axis=1) for k, a in zip(keys, masks)], axis=0
    )
    scores = lax.dot_general(ka, qa, (((1,), (1,)), ((), ())), preferred_element_type=jnp.float32)
    top = None
    for i in range(len(keys)):
        part = scores[i * block_len : (i + 1) * block_len]
        s_ref[i * block_len : (i + 1) * block_len, :] = part
        part = jnp.max(part.reshape(-1, 8, width), axis=0)
        top = part if top is None else jnp.maximum(top, part)
    t_ref[...] = jnp.broadcast_to(jnp.max(top, axis=0, keepdims=True), (8, width))


def weigh(top, s_ref, factor):
    total, weights = None, []
    step = 128
    width = s_ref.shape[1]
    for i in range(0, s_ref.shape[0], step):
        w = jnp.exp2((s_ref[i : i + step, :].reshape(-1, 8, width) - top) * factor)
        part = jnp.sum(w, axis=0)
        total = part if total is None else total + part
        weights.append(w.reshape(step, width).astype(jnp.bfloat16))
    return total, jnp.concatenate(weights, axis=0)


def gather_values(keys, vt_ref):
    return jnp.concatenate([vt_ref[k] for k in keys], axis=1)


def first_kernel(shards, query_heads, chosen_ref, k_hbm, v_hbm, q_hbm, *refs):
    (plan_ref, q_ref, kt_ref, vt_ref, m_ref, l_ref, acc_ref) = refs[:7]
    (raw, ask, asked, asked_s, plan_s, send, land, hot, aux, s_buf, t_buf) = refs[7:18]
    (load_sem, q_sem, ask_send, ask_recv, move_sem, plan_sem, block_send, block_recv) = refs[18:]
    me = lax.axis_index("ctx")
    tokens, heads, share, head_dim = q_ref.shape
    kv_heads, picks, blocks = chosen_ref.shape
    block_len = tokens // blocks
    width = block_len * share
    units = heads * blocks
    first_head = lax.axis_index("rep") * query_heads // (QUERY_HEADS // KEY_VALUE_HEADS)
    factor = head_dim**-0.5 * math.log2(math.e)
    loads = [pltpu.make_async_copy(src, raw.at[i], load_sem.at[i]) for i, src in enumerate((k_hbm, v_hbm))]
    for load in loads:
        load.start()
    q_load = pltpu.make_async_copy(q_hbm, q_ref, q_sem)
    q_load.start()
    barrier = pltpu.get_barrier_semaphore()
    for d in range(1, shards):
        pl.semaphore_signal(barrier, inc=1, device_id={"ctx": lax.rem(me + d, shards)}, device_id_type=MESH)

    lane = lax.broadcasted_iota(jnp.int32, (8, 128), 1)
    tiles = [jnp.zeros((8, 128), jnp.int32) for _ in range(1, shards)]
    base = me * blocks
    for h in range(heads):
        chosen = chosen_ref[first_head + h]
        local = (chosen >= base) & (chosen < base + blocks)
        slot = jnp.where(local, chosen - base + h * blocks, 0)
        for d in range(1, shards):
            start = (me - d) * blocks
            inside = (chosen >= start) & (chosen < start + blocks)
            first = jnp.min(jnp.where(inside, chosen, BIG), keepdims=True)
            later = inside & (chosen > first)
            second = jnp.min(jnp.where(later, chosen, BIG), keepdims=True)
            slot = jnp.where(inside, units + ((d - 1) * heads + h) * 2 + later.astype(jnp.int32), slot)
            for r, place in enumerate((first, second)):
                place = jnp.clip(place - start, 0, blocks - 1)
                tiles[d - 1] = jnp.where(lane == h * 2 + r, place, tiles[d - 1])
        rows = [chosen[k : k + 1, :] for k in range(picks)]
        slots = [slot[k : k + 1, :] for k in range(picks)]
        near = [(x >= base) & (x < base + blocks) for x in rows]
        is_local, is_remote = [], []
        for k in range(picks):
            fresh = jnp.ones(rows[k].shape, jnp.int32)
            for j in range(k):
                fresh = jnp.where(rows[j] == rows[k], 0, fresh)
            is_local.append(jnp.where(near[k], fresh, 0))
            is_remote.append(jnp.where(near[k], 0, fresh))
        local_count = functools.reduce(jnp.add, is_local)
        place_of, at_local, at_remote = [], jnp.zeros_like(local_count), local_count
        for k in range(picks):
            place = jnp.where(is_local[k] > 0, at_local, at_remote)
            place_of.append(jnp.where(is_local[k] + is_remote[k] > 0, place, picks))
            at_local = at_local + is_local[k]
            at_remote = at_remote + is_remote[k]
        for p in range(picks):
            total = jnp.zeros_like(local_count)
            for k in range(picks):
                total = jnp.where(place_of[k] == p, slots[k], total)
            plan_ref[h * PLAN_ROWS + p : h * PLAN_ROWS + p + 1, :] = total
        plan_ref[h * PLAN_ROWS + picks : h * PLAN_ROWS + picks + 1, :] = local_count
        plan_ref[h * PLAN_ROWS + picks + 1 : h * PLAN_ROWS + picks + 2, :] = at_remote
        for p in range(picks + 2, PLAN_ROWS):
            plan_ref[h * PLAN_ROWS + p : h * PLAN_ROWS + p + 1, :] = jnp.zeros_like(local_count)
    for d in range(1, shards):
        ask[d - 1] = tiles[d - 1]
    pl.semaphore_wait(barrier, shards - 1)

    def request(d):
        return pltpu.make_async_remote_copy(
            src_ref=ask.at[d - 1],
            dst_ref=asked.at[d - 1],
            send_sem=ask_send.at[d - 1],
            recv_sem=ask_recv.at[d - 1],
            device_id={"ctx": lax.rem(me - d + shards, shards)},
            device_id_type=MESH,
        )

    def deliver(d):
        return pltpu.make_async_remote_copy(
            src_ref=send.at[d - 1],
            dst_ref=land.at[d - 1],
            send_sem=block_send.at[d - 1],
            recv_sem=block_recv.at[d - 1],
            device_id={"ctx": lax.rem(me + d, shards)},
            device_id_type=MESH,
        )

    for d in range(1, shards):

        @pl.when(me >= d)
        def _(d=d):
            request(d).start()

    plan_copy = pltpu.make_async_copy(plan_ref, plan_s, plan_sem)
    plan_copy.start()
    fill_masks(hot, aux)
    for load in loads:
        load.wait()
    wide = kv_heads * block_len
    out_row = lax.broadcasted_iota(jnp.int32, (heads * block_len, wide), 0)
    in_row = lax.broadcasted_iota(jnp.int32, (heads * block_len, wide), 1)
    source = lax.rem(out_row, block_len) * kv_heads + first_head + lax.div(out_row, block_len)
    pick = jnp.where(source == in_row, 1.0, 0.0).astype(jnp.bfloat16)

    def split(b, carry):
        rows = pl.ds(pl.multiple_of(b * wide, wide), wide)
        parted = jnp.dot(pick, raw[0, rows, :], preferred_element_type=jnp.float32).astype(jnp.bfloat16)
        for h in range(heads):
            kt_ref[h * blocks + b] = parted[h * block_len : (h + 1) * block_len, :]
        parted = jnp.dot(pick, raw[1, rows, :], preferred_element_type=jnp.float32)
        for h in range(heads):
            vt_ref[h * blocks + b] = parted[h * block_len : (h + 1) * block_len, :].T.astype(jnp.bfloat16)
        return carry

    lax.fori_loop(0, blocks, split, 0)
    for d in range(1, shards):

        @pl.when(me + d < shards)
        def _(d=d):
            request(d).wait_recv()
            move = pltpu.make_async_copy(asked.at[d - 1], asked_s.at[d - 1], move_sem.at[d - 1])
            move.start()
            move.wait()
            for h in range(heads):
                for r in range(2):
                    place = asked_s[d - 1, 0, h * 2 + r] + h * blocks
                    for i, table in enumerate((kt_ref, vt_ref)):
                        send[d - 1, i, h * 2 + r] = table[place]
            deliver(d).start()

    plan_copy.wait()
    q_load.wait()
    half = picks // 2

    def slots_of(u):
        h, b = lax.rem(u, heads), lax.div(u, heads)
        near = plan_s[h * PLAN_ROWS + picks, b]
        keys = [jnp.where(p < near, plan_s[h * PLAN_ROWS + p, b], 0) for p in range(half)]
        masks = [jnp.where(p < near, CAUSAL if p == 0 else OPEN, CLOSED) for p in range(half)]
        return h, b, keys, masks

    def begin(u, buf):
        h, b, keys, masks = slots_of(u)
        q = q_ref[pl.ds(b * block_len, block_len), h].reshape(width, head_dim)
        score(q, keys, masks, hot, aux, kt_ref, s_buf.at[buf], t_buf.at[buf])

    def end(u, buf):
        h, b, keys, masks = slots_of(u)
        top = t_buf[buf]
        total, weights = weigh(top, s_buf.at[buf], factor)
        m_ref[u] = top
        l_ref[u] = total
        acc_ref[u] = jnp.dot(gather_values(keys, vt_ref), weights, preferred_element_type=jnp.float32)

    begin(0, 0)

    def pair(t, carry):
        u = 2 * t
        begin(jnp.minimum(u + 1, units - 1), 1)
        end(u, 0)
        begin(jnp.minimum(u + 2, units - 1), 0)
        end(jnp.minimum(u + 1, units - 1), 1)
        return carry

    lax.fori_loop(0, (units + 1) // 2, pair, 0)

    for d in range(1, shards):

        @pl.when(me >= d)
        def _(d=d):
            deliver(d).wait_recv()
            at = units + (d - 1) * heads * 2
            for j in range(heads * 2):
                kt_ref[at + j] = land[d - 1, 0, j]
                vt_ref[at + j] = land[d - 1, 1, j]

    for d in range(1, shards):

        @pl.when(me >= d)
        def _(d=d):
            request(d).wait_send()

        @pl.when(me + d < shards)
        def _(d=d):
            deliver(d).wait_send()


def second_kernel(picks, plan, q_ref, kt_ref, vt_ref, m_ref, l_ref, acc_ref, o_ref, items, held, held_acc, *work):
    hot, aux, s_buf, t_buf = work
    tokens, heads, share, head_dim = q_ref.shape
    units = acc_ref.shape[0]
    blocks = units // heads
    block_len = tokens // blocks
    width = block_len * share
    half = picks // 2
    factor = head_dim**-0.5 * math.log2(math.e)
    fill_masks(hot, aux)

    def lay(u, count):
        h, b = lax.rem(u, heads), lax.div(u, heads)
        at = jnp.minimum(plan[h * PLAN_ROWS + picks, b], half)
        items[0, count] = u
        items[1, count] = at
        items[2, count] = 0
        more = plan[h * PLAN_ROWS + picks + 1, b] - at > half
        items[0, count + 1] = u
        items[1, count + 1] = at + half
        items[2, count + 1] = 1
        return count + 1 + more.astype(jnp.int32)

    count = lax.fori_loop(0, units, lay, 0)
    for i in range(2):
        items[0, count + i] = units - 1
        items[1, count + i] = picks
        items[2, count + i] = 1

    def slots_of(i):
        u, at = items[0, i], items[1, i]
        h, b = lax.rem(u, heads), lax.div(u, heads)
        every = plan[h * PLAN_ROWS + picks + 1, b]
        inside = [at + p < every for p in range(half)]
        keys = [jnp.where(x, plan[h * PLAN_ROWS + jnp.minimum(at + p, picks - 1), b], 0) for p, x in enumerate(inside)]
        masks = [jnp.where(x, OPEN, CLOSED) for x in inside]
        return u, h, b, keys, masks

    def begin(i, buf):
        u, h, b, keys, masks = slots_of(i)
        q = q_ref[pl.ds(b * block_len, block_len), h].reshape(width, head_dim)
        score(q, keys, masks, hot, aux, kt_ref, s_buf.at[buf], t_buf.at[buf])

    def end(i, buf):
        u, h, b, keys, masks = slots_of(i)
        again = items[2, i] > 0
        old = jnp.where(again, held[0], m_ref[u])
        top = jnp.maximum(old, t_buf[buf])
        keep = jnp.exp2((old - top) * factor)
        total, weights = weigh(top, s_buf.at[buf], factor)
        total = jnp.where(again, held[1], l_ref[u]) * keep + total
        out = jnp.dot(gather_values(keys, vt_ref), weights, preferred_element_type=jnp.float32)
        out = jnp.where(again, held_acc[...], acc_ref[u]) * keep[:1] + out
        held[0] = top
        held[1] = total
        held_acc[...] = out
        out = out * (1.0 / jnp.sum(total, axis=0, keepdims=True))
        out = out.T.astype(o_ref.dtype)
        o_ref[pl.ds(b * block_len, block_len), h] = out.reshape(block_len, share, head_dim)

    begin(0, 0)

    def pair(t, carry):
        i = 2 * t
        begin(i + 1, 1)
        end(i, 0)
        begin(i + 2, 0)
        end(i + 1, 1)
        return carry

    lax.fori_loop(0, lax.div(count + 1, 2), pair, 0)


def on_device(queries, keys, values, chosen):
    tokens, query_heads, head_dim = queries.shape
    kv_heads, blocks, picks = chosen.shape
    block_len = tokens // blocks
    shards = lax.axis_size("ctx")
    heads = max(1, query_heads // (QUERY_HEADS // KEY_VALUE_HEADS))
    share = query_heads // heads
    width = block_len * share
    units = heads * blocks
    half = picks // 2
    partners = shards - 1
    held = units + partners * heads * 2
    vmem = pl.BlockSpec(memory_space=pltpu.VMEM)
    anywhere = pl.BlockSpec(memory_space=pltpu.HBM)
    q4 = jax.ShapeDtypeStruct((tokens, heads, share, head_dim), jnp.bfloat16)
    table = jax.ShapeDtypeStruct((held, block_len, head_dim), jnp.bfloat16)
    small = jax.ShapeDtypeStruct((units, 8, width), jnp.float32)
    large = jax.ShapeDtypeStruct((units, head_dim, width), jnp.float32)
    work = [
        pltpu.VMEM((width, block_len), jnp.bfloat16),
        pltpu.VMEM((3, block_len, block_len), jnp.bfloat16),
        pltpu.VMEM((2, half * block_len, width), jnp.float32),
        pltpu.VMEM((2, 8, width), jnp.float32),
    ]
    sent = (partners, 2, heads * 2, block_len, head_dim)
    q = queries.reshape(q4.shape)
    plan, q, kt, vt, m, l, acc = pl.pallas_call(
        functools.partial(first_kernel, shards, query_heads),
        out_shape=[jax.ShapeDtypeStruct((heads * PLAN_ROWS, blocks), jnp.int32), q4, table, table, small, small, large],
        in_specs=[vmem, anywhere, anywhere, anywhere],
        out_specs=[vmem] * 7,
        scratch_shapes=[
            pltpu.VMEM((2, tokens * kv_heads, head_dim), jnp.bfloat16),
            pltpu.VMEM((partners, 8, 128), jnp.int32),
            pltpu.VMEM((partners, 8, 128), jnp.int32),
            pltpu.SMEM((partners, 8, 128), jnp.int32),
            pltpu.SMEM((heads * PLAN_ROWS, blocks), jnp.int32),
            pltpu.VMEM(sent, jnp.bfloat16),
            pltpu.VMEM(sent, jnp.bfloat16),
            *work,
            pltpu.SemaphoreType.DMA((2,)),
            pltpu.SemaphoreType.DMA,
            pltpu.SemaphoreType.DMA((partners,)),
            pltpu.SemaphoreType.DMA((partners,)),
            pltpu.SemaphoreType.DMA((partners,)),
            pltpu.SemaphoreType.DMA,
            pltpu.SemaphoreType.DMA((partners,)),
            pltpu.SemaphoreType.DMA((partners,)),
        ],
        compiler_params=pltpu.CompilerParams(
            collective_id=0, has_side_effects=True, vmem_limit_bytes=14 * 1024 * 1024
        ),
    )(
        jnp.transpose(chosen, (0, 2, 1)),
        *(pltpu.with_memory_space_constraint(x, pltpu.HBM) for x in (keys.reshape(-1, head_dim), values.reshape(-1, head_dim), q)),
    )
    out = pl.pallas_call(
        functools.partial(second_kernel, picks),
        out_shape=q4,
        in_specs=[pl.BlockSpec(memory_space=pltpu.SMEM)] + [vmem] * 6,
        out_specs=vmem,
        scratch_shapes=[
            pltpu.SMEM((3, 2 * units + 3), jnp.int32),
            pltpu.VMEM((2, 8, width), jnp.float32),
            pltpu.VMEM((head_dim, width), jnp.float32),
            *work,
        ],
        compiler_params=pltpu.CompilerParams(vmem_limit_bytes=10 * 1024 * 1024),
    )(plan, q, kt, vt, m, l, acc)
    return out.reshape(tokens, query_heads, head_dim)


def solution(mesh):
    placed = (
        P(("groups", "ctx"), ("heads", "rep"), None),
        P(("groups", "ctx"), "heads", None),
        P(("groups", "ctx"), "heads", None),
        P("heads", ("groups", "ctx"), None),
    )
    return jax.shard_map(
        on_device,
        mesh=mesh,
        in_specs=placed,
        out_specs=P(("groups", "ctx"), ("heads", "rep"), None),
        check_vma=False,
    )
```

```python
import functools
import math

import jax
import jax.numpy as jnp
from jax import lax
from jax.experimental import pallas as pl
from jax.experimental.pallas import tpu as pltpu
from jax.sharding import PartitionSpec as P

QUERY_HEADS = 32
KEY_VALUE_HEADS = 8
REMOTE_BLOCK_MAX = 2
NEGATIVE = -1e30
BIG = 1 << 30
PLAN_ROWS = 16
OPEN, CAUSAL, CLOSED = 0, 1, 2
SPLIT = 4
ITEMS = 4
MESH = pl.DeviceIdType.MESH


def fill_masks(hot, aux):
    width, block_len = hot.shape
    row = lax.div(lax.broadcasted_iota(jnp.int32, (width, block_len), 0), width // block_len)
    lane = lax.broadcasted_iota(jnp.int32, (width, block_len), 1)
    hot[...] = jnp.where(row == lane, 1.0, 0.0).astype(jnp.bfloat16)
    key = lax.broadcasted_iota(jnp.int32, (block_len, block_len), 0)
    query = lax.broadcasted_iota(jnp.int32, (block_len, block_len), 1)
    aux[OPEN] = jnp.zeros((block_len, block_len), jnp.bfloat16)
    aux[CAUSAL] = jnp.where(key <= query, 0.0, NEGATIVE).astype(jnp.bfloat16)
    aux[CLOSED] = jnp.full((block_len, block_len), NEGATIVE, jnp.bfloat16)


def score(q, keys, masks, hot, aux, kt_ref, s_ref, t_ref):
    block_len = kt_ref.shape[1]
    width = q.shape[0]
    qa = jnp.concatenate([q, hot[...]], axis=1)
    ka = jnp.concatenate(
        [jnp.concatenate([kt_ref[k], aux[a]], axis=1) for k, a in zip(keys, masks)], axis=0
    )
    scores = lax.dot_general(ka, qa, (((1,), (1,)), ((), ())), preferred_element_type=jnp.float32)
    top = None
    for i in range(len(keys)):
        part = scores[i * block_len : (i + 1) * block_len]
        s_ref[i * block_len : (i + 1) * block_len, :] = part
        part = jnp.max(part.reshape(-1, 8, width), axis=0)
        top = part if top is None else jnp.maximum(top, part)
    t_ref[...] = jnp.broadcast_to(jnp.max(top, axis=0, keepdims=True), (8, width))


def weigh(top, s_ref, factor):
    total, weights = None, []
    step = 128
    width = s_ref.shape[1]
    for i in range(0, s_ref.shape[0], step):
        w = jnp.exp2((s_ref[i : i + step, :].reshape(-1, 8, width) - top) * factor)
        part = jnp.sum(w, axis=0)
        total = part if total is None else total + part
        weights.append(w.reshape(step, width).astype(jnp.bfloat16))
    return total, jnp.concatenate(weights, axis=0)


def gather_values(keys, vt_ref):
    return jnp.concatenate([vt_ref[k] for k in keys], axis=1)


def first_kernel(shards, query_heads, chosen_ref, k_hbm, v_hbm, q_hbm, *refs):
    (plan_ref, q_ref, kt_ref, vt_ref, m_ref, l_ref, acc_ref) = refs[:7]
    (raw, pick, ask, asked, asked_s, plan_s, send, land, hot, aux, s_buf, t_buf) = refs[7:19]
    (load_sem, q_sem, ask_send, ask_recv, move_sem, plan_sem, block_send, block_recv) = refs[19:]
    me = lax.axis_index("ctx")
    tokens, heads, share, head_dim = q_ref.shape
    kv_heads, picks, blocks = chosen_ref.shape
    block_len = tokens // blocks
    width = block_len * share
    units = heads * blocks
    first_head = lax.axis_index("rep") * query_heads // (QUERY_HEADS // KEY_VALUE_HEADS)
    factor = head_dim**-0.5 * math.log2(math.e)
    loads = [pltpu.make_async_copy(src, raw.at[i], load_sem.at[i]) for i, src in enumerate((k_hbm, v_hbm))]
    for load in loads:
        load.start()
    q_load = pltpu.make_async_copy(q_hbm, q_ref, q_sem)
    q_load.start()
    barrier = pltpu.get_barrier_semaphore()
    for d in range(1, shards):
        pl.semaphore_signal(barrier, inc=1, device_id={"ctx": lax.rem(me + d, shards)}, device_id_type=MESH)

    lane = lax.broadcasted_iota(jnp.int32, (8, 128), 1)
    tiles = [jnp.zeros((8, 128), jnp.int32) for _ in range(1, shards)]
    base = me * blocks
    for h in range(heads):
        chosen = chosen_ref[first_head + h]
        local = (chosen >= base) & (chosen < base + blocks)
        slot = jnp.where(local, chosen - base + h * blocks, 0)
        for d in range(1, shards):
            start = (me - d) * blocks
            inside = (chosen >= start) & (chosen < start + blocks)
            first = jnp.min(jnp.where(inside, chosen, BIG), keepdims=True)
            later = inside & (chosen > first)
            second = jnp.min(jnp.where(later, chosen, BIG), keepdims=True)
            slot = jnp.where(inside, units + ((d - 1) * heads + h) * 2 + later.astype(jnp.int32), slot)
            for r, place in enumerate((first, second)):
                place = jnp.clip(place - start, 0, blocks - 1)
                tiles[d - 1] = jnp.where(lane == h * 2 + r, place, tiles[d - 1])
        rows = [chosen[k : k + 1, :] for k in range(picks)]
        slots = [slot[k : k + 1, :] for k in range(picks)]
        near = [(x >= base) & (x < base + blocks) for x in rows]
        is_local, is_remote = [], []
        for k in range(picks):
            fresh = jnp.ones(rows[k].shape, jnp.int32)
            for j in range(k):
                fresh = jnp.where(rows[j] == rows[k], 0, fresh)
            is_local.append(jnp.where(near[k], fresh, 0))
            is_remote.append(jnp.where(near[k], 0, fresh))
        local_count = functools.reduce(jnp.add, is_local)
        place_of, at_local, at_remote = [], jnp.zeros_like(local_count), local_count
        for k in range(picks):
            place = jnp.where(is_local[k] > 0, at_local, at_remote)
            place_of.append(jnp.where(is_local[k] + is_remote[k] > 0, place, picks))
            at_local = at_local + is_local[k]
            at_remote = at_remote + is_remote[k]
        for p in range(picks):
            total = jnp.zeros_like(local_count)
            for k in range(picks):
                total = jnp.where(place_of[k] == p, slots[k], total)
            plan_ref[h * PLAN_ROWS + p : h * PLAN_ROWS + p + 1, :] = total
        plan_ref[h * PLAN_ROWS + picks : h * PLAN_ROWS + picks + 1, :] = local_count
        plan_ref[h * PLAN_ROWS + picks + 1 : h * PLAN_ROWS + picks + 2, :] = at_remote
        for p in range(picks + 2, PLAN_ROWS):
            plan_ref[h * PLAN_ROWS + p : h * PLAN_ROWS + p + 1, :] = jnp.zeros_like(local_count)
    for d in range(1, shards):
        ask[d - 1] = tiles[d - 1]
    pl.semaphore_wait(barrier, shards - 1)

    def request(d):
        return pltpu.make_async_remote_copy(
            src_ref=ask.at[d - 1],
            dst_ref=asked.at[d - 1],
            send_sem=ask_send.at[d - 1],
            recv_sem=ask_recv.at[d - 1],
            device_id={"ctx": lax.rem(me - d + shards, shards)},
            device_id_type=MESH,
        )

    def deliver(d):
        return pltpu.make_async_remote_copy(
            src_ref=send.at[d - 1],
            dst_ref=land.at[d - 1],
            send_sem=block_send.at[d - 1],
            recv_sem=block_recv.at[d - 1],
            device_id={"ctx": lax.rem(me + d, shards)},
            device_id_type=MESH,
        )

    for d in range(1, shards):

        @pl.when(me >= d)
        def _(d=d):
            request(d).start()

    plan_copy = pltpu.make_async_copy(plan_ref, plan_s, plan_sem)
    plan_copy.start()
    fill_masks(hot, aux)
    for load in loads:
        load.wait()
    wide = kv_heads * block_len
    out_row = lax.broadcasted_iota(jnp.int32, (heads * block_len, wide), 0)
    in_row = lax.broadcasted_iota(jnp.int32, (heads * block_len, wide), 1)
    source = lax.rem(out_row, block_len) * kv_heads + first_head + lax.div(out_row, block_len)
    pick[...] = jnp.where(source == in_row, 1.0, 0.0).astype(jnp.bfloat16)

    def parted(b, rows):
        both = jnp.concatenate([raw[0, b], raw[1, b]], axis=1)
        both = jnp.dot(pick[rows, :], both, preferred_element_type=jnp.float32)
        return both[:, :head_dim].astype(jnp.bfloat16), both[:, head_dim:]

    for d in range(1, shards):

        @pl.when(me + d < shards)
        def _(d=d):
            request(d).wait_recv()
            move = pltpu.make_async_copy(asked.at[d - 1], asked_s.at[d - 1], move_sem.at[d - 1])
            move.start()
            move.wait()
            for h in range(heads):
                for r in range(2):
                    place = asked_s[d - 1, 0, h * 2 + r]
                    k, v = parted(place, slice(h * block_len, (h + 1) * block_len))
                    send[d - 1, 0, h * 2 + r] = k
                    send[d - 1, 1, h * 2 + r] = v.T.astype(jnp.bfloat16)
            deliver(d).start()

    def split(t, carry):
        for j in range(SPLIT):
            b = jnp.minimum(t * SPLIT + j, blocks - 1)
            k, v = parted(b, slice(0, heads * block_len))
            for h in range(heads):
                rows = slice(h * block_len, (h + 1) * block_len)
                kt_ref[h * blocks + b] = k[rows, :]
                vt_ref[h * blocks + b] = v[rows, :].T.astype(jnp.bfloat16)
        return carry

    lax.fori_loop(0, pl.cdiv(blocks, SPLIT), split, 0)
    plan_copy.wait()
    q_load.wait()
    half = picks // 2

    def slots_of(u):
        h, b = lax.rem(u, heads), lax.div(u, heads)
        near = plan_s[h * PLAN_ROWS + picks, b]
        keys = [jnp.where(p < near, plan_s[h * PLAN_ROWS + p, b], 0) for p in range(half)]
        masks = [jnp.where(p < near, CAUSAL if p == 0 else OPEN, CLOSED) for p in range(half)]
        return h, b, keys, masks

    def begin(u, buf):
        h, b, keys, masks = slots_of(u)
        q = q_ref[pl.ds(b * block_len, block_len), h].reshape(width, head_dim)
        score(q, keys, masks, hot, aux, kt_ref, s_buf.at[buf], t_buf.at[buf])

    def end(u, buf):
        h, b, keys, masks = slots_of(u)
        top = t_buf[buf]
        total, weights = weigh(top, s_buf.at[buf], factor)
        m_ref[u] = top
        l_ref[u] = total
        acc_ref[u] = jnp.dot(gather_values(keys, vt_ref), weights, preferred_element_type=jnp.float32)

    begin(0, 0)

    def several(t, carry):
        u = ITEMS * t
        for j in range(ITEMS):
            begin(jnp.minimum(u + j + 1, units - 1), (j + 1) % 2)
            end(jnp.minimum(u + j, units - 1), j % 2)
        return carry

    lax.fori_loop(0, pl.cdiv(units, ITEMS), several, 0)

    for d in range(1, shards):

        @pl.when(me >= d)
        def _(d=d):
            deliver(d).wait_recv()
            at = units + (d - 1) * heads * 2
            for j in range(heads * 2):
                kt_ref[at + j] = land[d - 1, 0, j]
                vt_ref[at + j] = land[d - 1, 1, j]

    for d in range(1, shards):

        @pl.when(me >= d)
        def _(d=d):
            request(d).wait_send()

        @pl.when(me + d < shards)
        def _(d=d):
            deliver(d).wait_send()


def second_kernel(picks, plan, q_ref, kt_ref, vt_ref, m_ref, l_ref, acc_ref, o_hbm, items, held, held_acc, o_buf, o_sem, *work):
    hot, aux, s_buf, t_buf = work
    tokens, heads, share, head_dim = q_ref.shape
    units = acc_ref.shape[0]
    blocks = units // heads
    block_len = tokens // blocks
    width = block_len * share
    half = picks // 2
    factor = head_dim**-0.5 * math.log2(math.e)
    fill_masks(hot, aux)

    def lay(u, count):
        h, b = lax.rem(u, heads), lax.div(u, heads)
        at = jnp.minimum(plan[h * PLAN_ROWS + picks, b], half)
        items[0, count] = u
        items[1, count] = at
        items[2, count] = 0
        more = plan[h * PLAN_ROWS + picks + 1, b] - at > half
        items[0, count + 1] = u
        items[1, count + 1] = at + half
        items[2, count + 1] = 1
        return count + 1 + more.astype(jnp.int32)

    count = lax.fori_loop(0, units, lay, 0)
    for i in range(2):
        items[0, count + i] = units - 1
        items[1, count + i] = picks
        items[2, count + i] = 1

    def slots_of(i):
        u, at = items[0, i], items[1, i]
        h, b = lax.rem(u, heads), lax.div(u, heads)
        every = plan[h * PLAN_ROWS + picks + 1, b]
        inside = [at + p < every for p in range(half)]
        keys = [jnp.where(x, plan[h * PLAN_ROWS + jnp.minimum(at + p, picks - 1), b], 0) for p, x in enumerate(inside)]
        masks = [jnp.where(x, OPEN, CLOSED) for x in inside]
        return u, h, b, keys, masks

    def begin(i, buf):
        u, h, b, keys, masks = slots_of(i)
        q = q_ref[pl.ds(b * block_len, block_len), h].reshape(width, head_dim)
        score(q, keys, masks, hot, aux, kt_ref, s_buf.at[buf], t_buf.at[buf])

    def end(i, buf):
        u, h, b, keys, masks = slots_of(i)
        again = items[2, i] > 0
        old = jnp.where(again, held[0], m_ref[u])
        top = jnp.maximum(old, t_buf[buf])
        keep = jnp.exp2((old - top) * factor)
        total, weights = weigh(top, s_buf.at[buf], factor)
        total = jnp.where(again, held[1], l_ref[u]) * keep + total
        out = jnp.dot(gather_values(keys, vt_ref), weights, preferred_element_type=jnp.float32)
        out = jnp.where(again, held_acc[...], acc_ref[u]) * keep[:1] + out
        held[0] = top
        held[1] = total
        held_acc[...] = out
        out = out * (1.0 / jnp.sum(total, axis=0, keepdims=True))
        out = out.T.astype(o_buf.dtype)
        o_buf[pl.ds(b * block_len, block_len), h] = out.reshape(block_len, share, head_dim)

    begin(0, 0)

    def several(step, first, t, sent):
        i = first + step * t
        for j in range(step):
            begin(i + j + 1, (j + 1) % 2)
            end(i + j, j % 2)
        done = lax.div(items[0, i + step], heads)

        def ship(b, carry):
            shipped(b).start()
            return carry

        lax.fori_loop(sent, done, ship, 0)
        return done

    def shipped(b):
        rows = pl.ds(b * block_len, block_len)
        return pltpu.make_async_copy(o_buf.at[rows], o_hbm.at[rows], o_sem)

    many = lax.div(count, ITEMS)
    sent = lax.fori_loop(0, many, functools.partial(several, ITEMS, 0), 0)
    rest = count - many * ITEMS
    sent = lax.fori_loop(0, lax.div(rest + 1, 2), functools.partial(several, 2, many * ITEMS), sent)

    def ship_rest(b, carry):
        shipped(b).start()
        return carry

    lax.fori_loop(sent, blocks, ship_rest, 0)
    pltpu.make_async_copy(o_buf, o_hbm, o_sem).wait()


def on_device(queries, keys, values, chosen):
    tokens, query_heads, head_dim = queries.shape
    kv_heads, blocks, picks = chosen.shape
    block_len = tokens // blocks
    shards = lax.axis_size("ctx")
    heads = max(1, query_heads // (QUERY_HEADS // KEY_VALUE_HEADS))
    share = query_heads // heads
    width = block_len * share
    units = heads * blocks
    half = picks // 2
    partners = shards - 1
    held = units + partners * heads * 2
    vmem = pl.BlockSpec(memory_space=pltpu.VMEM)
    anywhere = pl.BlockSpec(memory_space=pltpu.HBM)
    q4 = jax.ShapeDtypeStruct((tokens, heads, share, head_dim), jnp.bfloat16)
    table = jax.ShapeDtypeStruct((held, block_len, head_dim), jnp.bfloat16)
    small = jax.ShapeDtypeStruct((units, 8, width), jnp.float32)
    large = jax.ShapeDtypeStruct((units, head_dim, width), jnp.float32)
    work = [
        pltpu.VMEM((width, block_len), jnp.bfloat16),
        pltpu.VMEM((3, block_len, block_len), jnp.bfloat16),
        pltpu.VMEM((2, half * block_len, width), jnp.float32),
        pltpu.VMEM((2, 8, width), jnp.float32),
    ]
    sent = (partners, 2, heads * 2, block_len, head_dim)
    q = queries.reshape(q4.shape)
    flat = (blocks, block_len * kv_heads, head_dim)
    plan, q, kt, vt, m, l, acc = pl.pallas_call(
        functools.partial(first_kernel, shards, query_heads),
        out_shape=[jax.ShapeDtypeStruct((heads * PLAN_ROWS, blocks), jnp.int32), q4, table, table, small, small, large],
        in_specs=[vmem, anywhere, anywhere, anywhere],
        out_specs=[vmem] * 7,
        scratch_shapes=[
            pltpu.VMEM((2, blocks, block_len * kv_heads, head_dim), jnp.bfloat16),
            pltpu.VMEM((heads * block_len, block_len * kv_heads), jnp.bfloat16),
            pltpu.VMEM((partners, 8, 128), jnp.int32),
            pltpu.VMEM((partners, 8, 128), jnp.int32),
            pltpu.SMEM((partners, 8, 128), jnp.int32),
            pltpu.SMEM((heads * PLAN_ROWS, blocks), jnp.int32),
            pltpu.VMEM(sent, jnp.bfloat16),
            pltpu.VMEM(sent, jnp.bfloat16),
            *work,
            pltpu.SemaphoreType.DMA((2,)),
            pltpu.SemaphoreType.DMA,
            pltpu.SemaphoreType.DMA((partners,)),
            pltpu.SemaphoreType.DMA((partners,)),
            pltpu.SemaphoreType.DMA((partners,)),
            pltpu.SemaphoreType.DMA,
            pltpu.SemaphoreType.DMA((partners,)),
            pltpu.SemaphoreType.DMA((partners,)),
        ],
        compiler_params=pltpu.CompilerParams(
            collective_id=0, has_side_effects=True, vmem_limit_bytes=14 * 1024 * 1024
        ),
    )(
        jnp.transpose(chosen, (0, 2, 1)),
        *(pltpu.with_memory_space_constraint(x, pltpu.HBM) for x in (keys.reshape(flat), values.reshape(flat), q)),
    )
    out = pl.pallas_call(
        functools.partial(second_kernel, picks),
        out_shape=q4,
        in_specs=[pl.BlockSpec(memory_space=pltpu.SMEM)] + [vmem] * 6,
        out_specs=anywhere,
        scratch_shapes=[
            pltpu.SMEM((3, 2 * units + ITEMS), jnp.int32),
            pltpu.VMEM((2, 8, width), jnp.float32),
            pltpu.VMEM((head_dim, width), jnp.float32),
            pltpu.VMEM(q4.shape, jnp.bfloat16),
            pltpu.SemaphoreType.DMA,
            *work,
        ],
        compiler_params=pltpu.CompilerParams(vmem_limit_bytes=10 * 1024 * 1024),
    )(plan, q, kt, vt, m, l, acc)
    return out.reshape(tokens, query_heads, head_dim)


def solution(mesh):
    placed = (
        P(("groups", "ctx"), ("heads", "rep"), None),
        P(("groups", "ctx"), "heads", None),
        P(("groups", "ctx"), "heads", None),
        P("heads", ("groups", "ctx"), None),
    )
    return jax.shard_map(
        on_device,
        mesh=mesh,
        in_specs=placed,
        out_specs=P(("groups", "ctx"), ("heads", "rep"), None),
        check_vma=False,
    )
```

```python
import functools
import math

import jax
import jax.numpy as jnp
from jax import lax
from jax.experimental import pallas as pl
from jax.experimental.pallas import tpu as pltpu
from jax.sharding import PartitionSpec as P

QUERY_HEADS = 32
KEY_VALUE_HEADS = 8
REMOTE_BLOCK_MAX = 2
NEGATIVE = -1e30
BIG = 1 << 30
PLAN_ROWS = 16
SPLIT = 4
ITEMS = 4
MESH = pl.DeviceIdType.MESH


def scaled_pair(k, factor):
    k = k * factor
    high = k.astype(jnp.bfloat16)
    low = (k - high.astype(jnp.float32)).astype(jnp.bfloat16)
    return jnp.concatenate([high, low], axis=1)


def score(q, keys, opens, causal, kt_ref, s_ref, t_ref):
    block_len = kt_ref.shape[1]
    width = q.shape[0]
    qa = jnp.concatenate([q, q], axis=1)
    ka = jnp.concatenate([kt_ref[k] for k in keys], axis=0)
    scores = lax.dot_general(ka, qa, (((1,), (1,)), ((), ())), preferred_element_type=jnp.float32)
    top = None
    for i, is_open in enumerate(opens):
        part = scores[i * block_len : (i + 1) * block_len]
        if causal and i == 0:
            key = lax.broadcasted_iota(jnp.int32, part.shape, 0)
            query = lax.div(lax.broadcasted_iota(jnp.int32, part.shape, 1), width // block_len)
            part = jnp.where(key <= query, part, NEGATIVE)
        s_ref[i * block_len : (i + 1) * block_len, :] = part
        part = jnp.max(part.reshape(-1, 8, width), axis=0)
        part = jnp.where(is_open, part, NEGATIVE)
        top = part if top is None else jnp.maximum(top, part)
    t_ref[...] = jnp.broadcast_to(jnp.max(top, axis=0, keepdims=True), (8, width))


def weigh(top, opens, block_len, s_ref):
    weights = []
    width = s_ref.shape[1]
    for i, is_open in enumerate(opens):
        less = jnp.where(is_open, top, -NEGATIVE)
        w = jnp.exp2(s_ref[i * block_len : (i + 1) * block_len, :].reshape(-1, 8, width) - less)
        weights.append(w.reshape(block_len, width).astype(jnp.bfloat16))
    return jnp.concatenate(weights, axis=0)


def weighted(keys, vt_ref, weights):
    head_dim = vt_ref.shape[1]
    values = jnp.concatenate([vt_ref[k] for k in keys], axis=1)
    values = jnp.concatenate([values, jnp.ones((16, values.shape[1]), values.dtype)], axis=0)
    out = jnp.dot(values, weights, preferred_element_type=jnp.float32)
    return out[:head_dim], out[head_dim : head_dim + 8]


def first_kernel(shards, query_heads, chosen_hbm, k_hbm, v_hbm, q_hbm, *refs):
    (plan_ref, q_ref, kt_ref, vt_ref, m_ref, l_ref, acc_ref) = refs[:7]
    (chosen_ref, raw, pick, ask, asked, plan_s, send, land, s_buf, t_buf) = refs[7:17]
    (chosen_sem, load_sem, q_sem, ask_send, ask_recv, plan_sem, block_send, block_recv) = refs[17:]
    me = lax.axis_index("ctx")
    tokens, heads, share, head_dim = q_ref.shape
    kv_heads, picks, blocks = chosen_ref.shape
    chosen_load = pltpu.make_async_copy(chosen_hbm, chosen_ref, chosen_sem)
    chosen_load.start()
    block_len = tokens // blocks
    width = block_len * share
    units = heads * blocks
    first_head = lax.axis_index("rep") * query_heads // (QUERY_HEADS // KEY_VALUE_HEADS)
    factor = head_dim**-0.5 * math.log2(math.e)
    barrier = pltpu.get_barrier_semaphore()
    for d in range(1, shards):
        pl.semaphore_signal(barrier, inc=1, device_id={"ctx": lax.rem(me + d, shards)}, device_id_type=MESH)
    loads = [pltpu.make_async_copy(src, raw.at[i], load_sem.at[i]) for i, src in enumerate((k_hbm, v_hbm))]
    for load in loads:
        load.start()
    q_load = pltpu.make_async_copy(q_hbm, q_ref, q_sem)

    lane = lax.broadcasted_iota(jnp.int32, (8, 128), 1)
    tiles = [jnp.zeros((8, 128), jnp.int32) for _ in range(1, shards)]
    base = me * blocks
    slot_of = []
    chosen_load.wait()
    for h in range(heads):
        chosen = chosen_ref[first_head + h]
        local = (chosen >= base) & (chosen < base + blocks)
        slot = jnp.where(local, chosen - base + h * blocks, 0)
        for d in range(1, shards):
            start = (me - d) * blocks
            inside = (chosen >= start) & (chosen < start + blocks)
            first = jnp.min(jnp.where(inside, chosen, BIG), keepdims=True)
            later = inside & (chosen > first)
            second = jnp.min(jnp.where(later, chosen, BIG), keepdims=True)
            slot = jnp.where(inside, units + ((d - 1) * heads + h) * 2 + later.astype(jnp.int32), slot)
            for r, place in enumerate((first, second)):
                place = jnp.clip(place - start, 0, blocks - 1)
                tiles[d - 1] = jnp.where(lane == h * 2 + r, place, tiles[d - 1])
        slot_of.append((chosen, slot))
    for d in range(1, shards):
        ask[d - 1] = tiles[d - 1]
    pl.semaphore_wait(barrier, shards - 1)

    def request(d):
        return pltpu.make_async_remote_copy(
            src_ref=ask.at[d - 1],
            dst_ref=asked.at[d - 1],
            send_sem=ask_send.at[d - 1],
            recv_sem=ask_recv.at[d - 1],
            device_id={"ctx": lax.rem(me - d + shards, shards)},
            device_id_type=MESH,
        )

    def deliver(d):
        return pltpu.make_async_remote_copy(
            src_ref=send.at[d - 1],
            dst_ref=land.at[d - 1],
            send_sem=block_send.at[d - 1],
            recv_sem=block_recv.at[d - 1],
            device_id={"ctx": lax.rem(me + d, shards)},
            device_id_type=MESH,
        )

    for d in range(1, shards):

        @pl.when(me >= d)
        def _(d=d):
            request(d).start()

    q_load.start()
    for h, (chosen, slot) in enumerate(slot_of):
        rows = [chosen[k : k + 1, :] for k in range(picks)]
        slots = [slot[k : k + 1, :] for k in range(picks)]
        near = [(x >= base) & (x < base + blocks) for x in rows]
        is_local, is_remote = [], []
        for k in range(picks):
            fresh = jnp.ones(rows[k].shape, jnp.int32)
            for j in range(k):
                fresh = jnp.where(rows[j] == rows[k], 0, fresh)
            is_local.append(jnp.where(near[k], fresh, 0))
            is_remote.append(jnp.where(near[k], 0, fresh))
        local_count = functools.reduce(jnp.add, is_local)
        place_of, at_local, at_remote = [], jnp.zeros_like(local_count), local_count
        for k in range(picks):
            place = jnp.where(is_local[k] > 0, at_local, at_remote)
            place_of.append(jnp.where(is_local[k] + is_remote[k] > 0, place, picks))
            at_local = at_local + is_local[k]
            at_remote = at_remote + is_remote[k]
        for p in range(picks):
            total = jnp.zeros_like(local_count)
            for k in range(picks):
                total = jnp.where(place_of[k] == p, slots[k], total)
            plan_ref[h * PLAN_ROWS + p : h * PLAN_ROWS + p + 1, :] = total
        plan_ref[h * PLAN_ROWS + picks : h * PLAN_ROWS + picks + 1, :] = local_count
        plan_ref[h * PLAN_ROWS + picks + 1 : h * PLAN_ROWS + picks + 2, :] = at_remote
        for p in range(picks + 2, PLAN_ROWS):
            plan_ref[h * PLAN_ROWS + p : h * PLAN_ROWS + p + 1, :] = jnp.zeros_like(local_count)
    plan_copy = pltpu.make_async_copy(plan_ref, plan_s, plan_sem)
    plan_copy.start()
    for load in loads:
        load.wait()
    wide = kv_heads * block_len
    out_row = lax.broadcasted_iota(jnp.int32, (heads * block_len, wide), 0)
    in_row = lax.broadcasted_iota(jnp.int32, (heads * block_len, wide), 1)
    source = lax.rem(out_row, block_len) * kv_heads + first_head + lax.div(out_row, block_len)
    pick[...] = jnp.where(source == in_row, 1.0, 0.0).astype(jnp.bfloat16)

    def parted(b, rows):
        both = jnp.concatenate([raw[0, b], raw[1, b]], axis=1)
        both = jnp.dot(pick[rows, :], both, preferred_element_type=jnp.float32)
        return both[:, :head_dim], both[:, head_dim:]

    for d in range(shards - 1, 0, -1):

        @pl.when(me + d < shards)
        def _(d=d):
            request(d).wait_recv()
            places = asked[d - 1]
            for h in range(heads):
                for r in range(2):
                    place = jnp.max(jnp.where(lane == h * 2 + r, places, 0))
                    k, v = parted(place, slice(h * block_len, (h + 1) * block_len))
                    send[d - 1, 0, h * 2 + r] = k.astype(jnp.bfloat16)
                    send[d - 1, 1, h * 2 + r] = v.T.astype(jnp.bfloat16)
            deliver(d).start()

    def split(t, carry):
        for j in range(SPLIT):
            b = jnp.minimum(t * SPLIT + j, blocks - 1)
            k, v = parted(b, slice(0, heads * block_len))
            for h in range(heads):
                rows = slice(h * block_len, (h + 1) * block_len)
                kt_ref[h * blocks + b] = scaled_pair(k[rows, :], factor)
                vt_ref[h * blocks + b] = v[rows, :].T.astype(jnp.bfloat16)
        return carry

    lax.fori_loop(0, pl.cdiv(blocks, SPLIT), split, 0)
    plan_copy.wait()
    q_load.wait()
    half = picks // 2

    def slots_of(u):
        h, b = lax.rem(u, heads), lax.div(u, heads)
        near = plan_s[h * PLAN_ROWS + picks, b]
        keys = [jnp.where(p < near, plan_s[h * PLAN_ROWS + p, b], 0) for p in range(half)]
        return h, b, keys, [p < near for p in range(half)]

    def begin(u, buf):
        h, b, keys, opens = slots_of(u)
        q = q_ref[pl.ds(b * block_len, block_len), h].reshape(width, head_dim)
        score(q, keys, opens, True, kt_ref, s_buf.at[buf], t_buf.at[buf])

    def end(u, buf):
        h, b, keys, opens = slots_of(u)
        top = t_buf[buf]
        weights = weigh(top, opens, block_len, s_buf.at[buf])
        m_ref[u] = top
        acc_ref[u], l_ref[u] = weighted(keys, vt_ref, weights)

    begin(0, 0)

    def several(t, carry):
        u = ITEMS * t
        for j in range(ITEMS):
            begin(jnp.minimum(u + j + 1, units - 1), (j + 1) % 2)
            end(jnp.minimum(u + j, units - 1), j % 2)
        return carry

    lax.fori_loop(0, pl.cdiv(units, ITEMS), several, 0)

    for d in range(1, shards):

        @pl.when(me >= d)
        def _(d=d):
            deliver(d).wait_recv()
            at = units + (d - 1) * heads * 2
            for j in range(heads * 2):
                kt_ref[at + j] = scaled_pair(land[d - 1, 0, j].astype(jnp.float32), factor)
                vt_ref[at + j] = land[d - 1, 1, j]

    for d in range(1, shards):

        @pl.when(me >= d)
        def _(d=d):
            request(d).wait_send()

        @pl.when(me + d < shards)
        def _(d=d):
            deliver(d).wait_send()


def second_kernel(picks, plan, q_ref, kt_ref, vt_ref, m_ref, l_ref, acc_ref, o_hbm, items, held, held_acc, o_buf, o_sem, *work):
    s_buf, t_buf = work
    tokens, heads, share, head_dim = q_ref.shape
    units = acc_ref.shape[0]
    blocks = units // heads
    block_len = tokens // blocks
    width = block_len * share
    half = picks // 2

    def lay(u, count):
        h, b = lax.rem(u, heads), lax.div(u, heads)
        at = jnp.minimum(plan[h * PLAN_ROWS + picks, b], half)
        items[0, count] = u
        items[1, count] = at
        items[2, count] = 0
        more = plan[h * PLAN_ROWS + picks + 1, b] - at > half
        items[0, count + 1] = u
        items[1, count + 1] = at + half
        items[2, count + 1] = 1
        return count + 1 + more.astype(jnp.int32)

    count = lax.fori_loop(0, units, lay, 0)
    for i in range(2):
        items[0, count + i] = units - 1
        items[1, count + i] = picks
        items[2, count + i] = 1

    def slots_of(i):
        u, at = items[0, i], items[1, i]
        h, b = lax.rem(u, heads), lax.div(u, heads)
        every = plan[h * PLAN_ROWS + picks + 1, b]
        inside = [at + p < every for p in range(half)]
        keys = [jnp.where(x, plan[h * PLAN_ROWS + jnp.minimum(at + p, picks - 1), b], 0) for p, x in enumerate(inside)]
        return u, h, b, keys, inside

    def begin(i, buf):
        u, h, b, keys, opens = slots_of(i)
        q = q_ref[pl.ds(b * block_len, block_len), h].reshape(width, head_dim)
        score(q, keys, opens, False, kt_ref, s_buf.at[buf], t_buf.at[buf])

    def end(i, buf):
        u, h, b, keys, opens = slots_of(i)
        again = items[2, i] > 0
        old = jnp.where(again, held[0], m_ref[u])
        top = jnp.maximum(old, t_buf[buf])
        keep = jnp.exp2(old - top)
        weights = weigh(top, opens, block_len, s_buf.at[buf])
        out, total = weighted(keys, vt_ref, weights)
        total = jnp.where(again, held[1], l_ref[u]) * keep + total
        out = jnp.where(again, held_acc[...], acc_ref[u]) * keep[:1] + out
        held[0] = top
        held[1] = total
        held_acc[...] = out

    def finish(i):
        u = items[0, jnp.maximum(i, 0)]
        h, b = lax.rem(u, heads), lax.div(u, heads)
        out = held_acc[...] * (1.0 / held[1])[:1]
        out = out.T.astype(o_buf.dtype)
        o_buf[pl.ds(b * block_len, block_len), h] = out.reshape(block_len, share, head_dim)

    begin(0, 0)

    def several(step, first, t, sent):
        i = first + step * t
        for j in range(step):
            finish(i + j - 1)
            begin(i + j + 1, (j + 1) % 2)
            end(i + j, j % 2)
        done = lax.div(items[0, i + step - 1], heads)

        def ship(b, carry):
            shipped(b).start()
            return carry

        lax.fori_loop(sent, done, ship, 0)
        return done

    def shipped(b):
        rows = pl.ds(b * block_len, block_len)
        return pltpu.make_async_copy(o_buf.at[rows], o_hbm.at[rows], o_sem)

    many = lax.div(count, ITEMS)
    sent = lax.fori_loop(0, many, functools.partial(several, ITEMS, 0), 0)
    rest = count - many * ITEMS
    pairs = lax.div(rest + 1, 2)
    sent = lax.fori_loop(0, pairs, functools.partial(several, 2, many * ITEMS), sent)
    finish(many * ITEMS + 2 * pairs - 1)

    def ship_rest(b, carry):
        shipped(b).start()
        return carry

    lax.fori_loop(sent, blocks, ship_rest, 0)
    pltpu.make_async_copy(o_buf, o_hbm, o_sem).wait()


def on_device(queries, keys, values, chosen):
    tokens, query_heads, head_dim = queries.shape
    kv_heads, blocks, picks = chosen.shape
    block_len = tokens // blocks
    shards = lax.axis_size("ctx")
    heads = max(1, query_heads // (QUERY_HEADS // KEY_VALUE_HEADS))
    share = query_heads // heads
    width = block_len * share
    units = heads * blocks
    half = picks // 2
    partners = shards - 1
    held = units + partners * heads * 2
    vmem = pl.BlockSpec(memory_space=pltpu.VMEM)
    anywhere = pl.BlockSpec(memory_space=pltpu.HBM)
    q4 = jax.ShapeDtypeStruct((tokens, heads, share, head_dim), jnp.bfloat16)
    k_table = jax.ShapeDtypeStruct((held, block_len, 2 * head_dim), jnp.bfloat16)
    v_table = jax.ShapeDtypeStruct((held, head_dim, block_len), jnp.bfloat16)
    small = jax.ShapeDtypeStruct((units, 8, width), jnp.float32)
    large = jax.ShapeDtypeStruct((units, head_dim, width), jnp.float32)
    work = [
        pltpu.VMEM((2, half * block_len, width), jnp.float32),
        pltpu.VMEM((2, 8, width), jnp.float32),
    ]
    sent = (partners, 2, heads * 2, block_len, head_dim)
    q = queries.reshape(q4.shape)
    flat = (blocks, block_len * kv_heads, head_dim)
    plan, q, kt, vt, m, l, acc = pl.pallas_call(
        functools.partial(first_kernel, shards, query_heads),
        out_shape=[jax.ShapeDtypeStruct((heads * PLAN_ROWS, blocks), jnp.int32), q4, k_table, v_table, small, small, large],
        in_specs=[anywhere] * 4,
        out_specs=[vmem] * 7,
        scratch_shapes=[
            pltpu.VMEM((kv_heads, picks, blocks), jnp.int32),
            pltpu.VMEM((2, blocks, block_len * kv_heads, head_dim), jnp.bfloat16),
            pltpu.VMEM((heads * block_len, block_len * kv_heads), jnp.bfloat16),
            pltpu.VMEM((partners, 8, 128), jnp.int32),
            pltpu.VMEM((partners, 8, 128), jnp.int32),
            pltpu.SMEM((heads * PLAN_ROWS, blocks), jnp.int32),
            pltpu.VMEM(sent, jnp.bfloat16),
            pltpu.VMEM(sent, jnp.bfloat16),
            *work,
            pltpu.SemaphoreType.DMA,
            pltpu.SemaphoreType.DMA((2,)),
            pltpu.SemaphoreType.DMA,
            pltpu.SemaphoreType.DMA((partners,)),
            pltpu.SemaphoreType.DMA((partners,)),
            pltpu.SemaphoreType.DMA,
            pltpu.SemaphoreType.DMA((partners,)),
            pltpu.SemaphoreType.DMA((partners,)),
        ],
        compiler_params=pltpu.CompilerParams(
            collective_id=0, has_side_effects=True, vmem_limit_bytes=14 * 1024 * 1024
        ),
    )(
        *(pltpu.with_memory_space_constraint(x, pltpu.HBM) for x in (jnp.transpose(chosen, (0, 2, 1)), keys.reshape(flat), values.reshape(flat), q)),
    )
    out = pl.pallas_call(
        functools.partial(second_kernel, picks),
        out_shape=q4,
        in_specs=[pl.BlockSpec(memory_space=pltpu.SMEM)] + [vmem] * 6,
        out_specs=anywhere,
        scratch_shapes=[
            pltpu.SMEM((3, 2 * units + ITEMS), jnp.int32),
            pltpu.VMEM((2, 8, width), jnp.float32),
            pltpu.VMEM((head_dim, width), jnp.float32),
            pltpu.VMEM(q4.shape, jnp.bfloat16),
            pltpu.SemaphoreType.DMA,
            *work,
        ],
        compiler_params=pltpu.CompilerParams(vmem_limit_bytes=10 * 1024 * 1024),
    )(plan, q, kt, vt, m, l, acc)
    return out.reshape(tokens, query_heads, head_dim)


def solution(mesh):
    placed = (
        P(("groups", "ctx"), ("heads", "rep"), None),
        P(("groups", "ctx"), "heads", None),
        P(("groups", "ctx"), "heads", None),
        P("heads", ("groups", "ctx"), None),
    )
    return jax.shard_map(
        on_device,
        mesh=mesh,
        in_specs=placed,
        out_specs=P(("groups", "ctx"), ("heads", "rep"), None),
        check_vma=False,
    )
```

```python
import functools
import math

import jax
import jax.numpy as jnp
from jax import lax
from jax.experimental import pallas as pl
from jax.experimental.pallas import tpu as pltpu
from jax.sharding import PartitionSpec as P

QUERY_HEADS = 32
KEY_VALUE_HEADS = 8
REMOTE_BLOCK_MAX = 2
NEGATIVE = -1e30
BIG = 1 << 30
PLAN_ROWS = 16
SPLIT = 4
ITEMS = 8
BUFFERS = 2
MESH = pl.DeviceIdType.MESH


def scaled_pair(k, factor):
    k = k * factor
    high = k.astype(jnp.bfloat16)
    low = (k - high.astype(jnp.float32)).astype(jnp.bfloat16)
    return jnp.concatenate([high, low], axis=1)


def score(q, keys, opens, causal, kt_ref, s_ref, t_ref):
    block_len = kt_ref.shape[1]
    width = q.shape[0]
    qa = jnp.concatenate([q, q], axis=1)
    ka = jnp.concatenate([kt_ref[k] for k in keys], axis=0)
    scores = lax.dot_general(ka, qa, (((1,), (1,)), ((), ())), preferred_element_type=jnp.float32)
    top = None
    for i, is_open in enumerate(opens):
        part = scores[i * block_len : (i + 1) * block_len]
        if causal and i == 0:
            key = lax.broadcasted_iota(jnp.int32, part.shape, 0)
            query = lax.div(lax.broadcasted_iota(jnp.int32, part.shape, 1), width // block_len)
            part = jnp.where(key <= query, part, NEGATIVE)
        s_ref[i * block_len : (i + 1) * block_len, :] = part
        part = jnp.max(part.reshape(-1, 8, width), axis=0)
        part = jnp.where(is_open, part, NEGATIVE)
        top = part if top is None else jnp.maximum(top, part)
    t_ref[...] = jnp.broadcast_to(jnp.max(top, axis=0, keepdims=True), (8, width))


def weigh(top, opens, block_len, s_ref):
    weights = []
    width = s_ref.shape[1]
    for i, is_open in enumerate(opens):
        less = jnp.where(is_open, top, -NEGATIVE)
        w = jnp.exp2(s_ref[i * block_len : (i + 1) * block_len, :].reshape(-1, 8, width) - less)
        weights.append(w.reshape(block_len, width).astype(jnp.bfloat16))
    return jnp.concatenate(weights, axis=0)


def weighted(keys, vt_ref, weights):
    head_dim = vt_ref.shape[1]
    values = jnp.concatenate([vt_ref[k] for k in keys], axis=1)
    values = jnp.concatenate([values, jnp.ones((16, values.shape[1]), values.dtype)], axis=0)
    out = jnp.dot(values, weights, preferred_element_type=jnp.float32)
    return out[:head_dim], out[head_dim : head_dim + 8]


def first_kernel(shards, query_heads, chosen_hbm, k_hbm, v_hbm, q_hbm, *refs):
    (plan_ref, q_ref, kt_ref, vt_ref, m_ref, l_ref, acc_ref) = refs[:7]
    (chosen_ref, raw, pick, ask, asked, plan_s, send, land, s_buf, t_buf) = refs[7:17]
    (chosen_sem, load_sem, q_sem, ask_send, ask_recv, plan_sem, block_send, block_recv) = refs[17:]
    me = lax.axis_index("ctx")
    tokens, heads, share, head_dim = q_ref.shape
    kv_heads, picks, blocks = chosen_ref.shape
    chosen_load = pltpu.make_async_copy(chosen_hbm, chosen_ref, chosen_sem)
    chosen_load.start()
    block_len = tokens // blocks
    width = block_len * share
    units = heads * blocks
    first_head = lax.axis_index("rep") * query_heads // (QUERY_HEADS // KEY_VALUE_HEADS)
    factor = head_dim**-0.5 * math.log2(math.e)
    barrier = pltpu.get_barrier_semaphore()
    for d in range(1, shards):
        pl.semaphore_signal(barrier, inc=1, device_id={"ctx": lax.rem(me + d, shards)}, device_id_type=MESH)
    loads = [pltpu.make_async_copy(src, raw.at[i], load_sem.at[i]) for i, src in enumerate((k_hbm, v_hbm))]
    for load in loads:
        load.start()
    q_load = pltpu.make_async_copy(q_hbm, q_ref, q_sem)

    lane = lax.broadcasted_iota(jnp.int32, (8, 128), 1)
    tiles = [jnp.zeros((8, 128), jnp.int32) for _ in range(1, shards)]
    base = me * blocks
    slot_of = []
    chosen_load.wait()
    for h in range(heads):
        chosen = chosen_ref[first_head + h]
        local = (chosen >= base) & (chosen < base + blocks)
        slot = jnp.where(local, chosen - base + h * blocks, 0)
        for d in range(1, shards):
            start = (me - d) * blocks
            inside = (chosen >= start) & (chosen < start + blocks)
            first = jnp.min(jnp.where(inside, chosen, BIG), keepdims=True)
            later = inside & (chosen > first)
            second = jnp.min(jnp.where(later, chosen, BIG), keepdims=True)
            slot = jnp.where(inside, units + ((d - 1) * heads + h) * 2 + later.astype(jnp.int32), slot)
            for r, place in enumerate((first, second)):
                place = jnp.clip(place - start, 0, blocks - 1)
                tiles[d - 1] = jnp.where(lane == h * 2 + r, place, tiles[d - 1])
        slot_of.append((chosen, slot))
    for d in range(1, shards):
        ask[d - 1] = tiles[d - 1]
    pl.semaphore_wait(barrier, shards - 1)

    def request(d):
        return pltpu.make_async_remote_copy(
            src_ref=ask.at[d - 1],
            dst_ref=asked.at[d - 1],
            send_sem=ask_send.at[d - 1],
            recv_sem=ask_recv.at[d - 1],
            device_id={"ctx": lax.rem(me - d + shards, shards)},
            device_id_type=MESH,
        )

    def deliver(d):
        return pltpu.make_async_remote_copy(
            src_ref=send.at[d - 1],
            dst_ref=land.at[d - 1],
            send_sem=block_send.at[d - 1],
            recv_sem=block_recv.at[d - 1],
            device_id={"ctx": lax.rem(me + d, shards)},
            device_id_type=MESH,
        )

    for d in range(1, shards):

        @pl.when(me >= d)
        def _(d=d):
            request(d).start()

    q_load.start()
    for h, (chosen, slot) in enumerate(slot_of):
        rows = [chosen[k : k + 1, :] for k in range(picks)]
        slots = [slot[k : k + 1, :] for k in range(picks)]
        near = [(x >= base) & (x < base + blocks) for x in rows]
        is_local, is_remote = [], []
        for k in range(picks):
            fresh = jnp.ones(rows[k].shape, jnp.int32)
            for j in range(k):
                fresh = jnp.where(rows[j] == rows[k], 0, fresh)
            is_local.append(jnp.where(near[k], fresh, 0))
            is_remote.append(jnp.where(near[k], 0, fresh))
        local_count = functools.reduce(jnp.add, is_local)
        place_of, at_local, at_remote = [], jnp.zeros_like(local_count), local_count
        for k in range(picks):
            place = jnp.where(is_local[k] > 0, at_local, at_remote)
            place_of.append(jnp.where(is_local[k] + is_remote[k] > 0, place, picks))
            at_local = at_local + is_local[k]
            at_remote = at_remote + is_remote[k]
        for p in range(picks):
            total = jnp.zeros_like(local_count)
            for k in range(picks):
                total = jnp.where(place_of[k] == p, slots[k], total)
            plan_ref[h * PLAN_ROWS + p : h * PLAN_ROWS + p + 1, :] = total
        plan_ref[h * PLAN_ROWS + picks : h * PLAN_ROWS + picks + 1, :] = local_count
        plan_ref[h * PLAN_ROWS + picks + 1 : h * PLAN_ROWS + picks + 2, :] = at_remote
        for p in range(picks + 2, PLAN_ROWS):
            plan_ref[h * PLAN_ROWS + p : h * PLAN_ROWS + p + 1, :] = jnp.zeros_like(local_count)
    plan_copy = pltpu.make_async_copy(plan_ref, plan_s, plan_sem)
    plan_copy.start()
    for load in loads:
        load.wait()
    wide = kv_heads * block_len
    out_row = lax.broadcasted_iota(jnp.int32, (heads * block_len, wide), 0)
    in_row = lax.broadcasted_iota(jnp.int32, (heads * block_len, wide), 1)
    source = lax.rem(out_row, block_len) * kv_heads + first_head + lax.div(out_row, block_len)
    pick[...] = jnp.where(source == in_row, 1.0, 0.0).astype(jnp.bfloat16)

    def parted(b, rows):
        both = jnp.concatenate([raw[0, b], raw[1, b]], axis=1)
        both = jnp.dot(pick[rows, :], both, preferred_element_type=jnp.float32)
        return both[:, :head_dim], both[:, head_dim:]

    for d in range(shards - 1, 0, -1):

        @pl.when(me + d < shards)
        def _(d=d):
            request(d).wait_recv()
            places = asked[d - 1]
            for h in range(heads):
                for r in range(2):
                    place = jnp.max(jnp.where(lane == h * 2 + r, places, 0))
                    k, v = parted(place, slice(h * block_len, (h + 1) * block_len))
                    send[d - 1, 0, h * 2 + r] = k.astype(jnp.bfloat16)
                    send[d - 1, 1, h * 2 + r] = v.T.astype(jnp.bfloat16)
            deliver(d).start()

    def split(t, carry):
        for j in range(SPLIT):
            b = jnp.minimum(t * SPLIT + j, blocks - 1)
            k, v = parted(b, slice(0, heads * block_len))
            for h in range(heads):
                rows = slice(h * block_len, (h + 1) * block_len)
                kt_ref[h * blocks + b] = scaled_pair(k[rows, :], factor)
                vt_ref[h * blocks + b] = v[rows, :].T.astype(jnp.bfloat16)
        return carry

    lax.fori_loop(0, pl.cdiv(blocks, SPLIT), split, 0)
    plan_copy.wait()
    q_load.wait()
    half = picks // 2

    def slots_of(u):
        h, b = lax.rem(u, heads), lax.div(u, heads)
        near = plan_s[h * PLAN_ROWS + picks, b]
        keys = [jnp.where(p < near, plan_s[h * PLAN_ROWS + p, b], 0) for p in range(half)]
        return h, b, keys, [p < near for p in range(half)]

    def begin(u, buf):
        h, b, keys, opens = slots_of(u)
        q = q_ref[pl.ds(b * block_len, block_len), h].reshape(width, head_dim)
        score(q, keys, opens, True, kt_ref, s_buf.at[buf], t_buf.at[buf])

    def end(u, buf):
        h, b, keys, opens = slots_of(u)
        top = t_buf[buf]
        weights = weigh(top, opens, block_len, s_buf.at[buf])
        m_ref[u] = top
        acc_ref[u], l_ref[u] = weighted(keys, vt_ref, weights)

    begin(0, 0)

    def several(t, carry):
        u = ITEMS * t
        for j in range(ITEMS):
            begin(jnp.minimum(u + j + 1, units - 1), (j + 1) % BUFFERS)
            end(jnp.minimum(u + j, units - 1), j % BUFFERS)
        return carry

    lax.fori_loop(0, pl.cdiv(units, ITEMS), several, 0)

    for d in range(1, shards):

        @pl.when(me >= d)
        def _(d=d):
            deliver(d).wait_recv()
            at = units + (d - 1) * heads * 2
            for j in range(heads * 2):
                kt_ref[at + j] = scaled_pair(land[d - 1, 0, j].astype(jnp.float32), factor)
                vt_ref[at + j] = land[d - 1, 1, j]

    for d in range(1, shards):

        @pl.when(me >= d)
        def _(d=d):
            request(d).wait_send()

        @pl.when(me + d < shards)
        def _(d=d):
            deliver(d).wait_send()


def second_kernel(picks, plan, q_ref, kt_ref, vt_ref, m_ref, l_ref, acc_ref, o_hbm, items, held, held_acc, o_buf, o_sem, *work):
    s_buf, t_buf = work
    tokens, heads, share, head_dim = q_ref.shape
    units = acc_ref.shape[0]
    blocks = units // heads
    block_len = tokens // blocks
    width = block_len * share
    half = picks // 2

    def lay(b, count):
        for h in range(heads):
            at = jnp.minimum(plan[h * PLAN_ROWS + picks, b], half)
            more = plan[h * PLAN_ROWS + picks + 1, b] - at > half
            for j in range(2):
                items[0, count + j] = b * heads + h
                items[1, count + j] = at + j * half
                items[2, count + j] = j
            count = count + 1 + more.astype(jnp.int32)
        return count

    count = lax.fori_loop(0, blocks, lay, 0, unroll=4)
    for i in range(BUFFERS + 1):
        items[0, count + i] = units - 1
        items[1, count + i] = picks
        items[2, count + i] = 1

    def slots_of(i):
        u, at = items[0, i], items[1, i]
        h, b = lax.rem(u, heads), lax.div(u, heads)
        every = plan[h * PLAN_ROWS + picks + 1, b]
        inside = [at + p < every for p in range(half)]
        keys = [jnp.where(x, plan[h * PLAN_ROWS + jnp.minimum(at + p, picks - 1), b], 0) for p, x in enumerate(inside)]
        return u, h, b, keys, inside

    def begin(i, buf):
        u, h, b, keys, opens = slots_of(i)
        q = q_ref[pl.ds(b * block_len, block_len), h].reshape(width, head_dim)
        score(q, keys, opens, False, kt_ref, s_buf.at[buf], t_buf.at[buf])

    def end(i, buf):
        u, h, b, keys, opens = slots_of(i)
        again = items[2, i] > 0
        old = jnp.where(again, held[0], m_ref[u])
        top = jnp.maximum(old, t_buf[buf])
        keep = jnp.exp2(old - top)
        weights = weigh(top, opens, block_len, s_buf.at[buf])
        out, total = weighted(keys, vt_ref, weights)
        total = jnp.where(again, held[1], l_ref[u]) * keep + total
        out = jnp.where(again, held_acc[...], acc_ref[u]) * keep[:1] + out
        held[0] = top
        held[1] = total
        held_acc[...] = out

    def finish(i):
        u = items[0, jnp.maximum(i, 0)]
        h, b = lax.rem(u, heads), lax.div(u, heads)
        out = held_acc[...] * (1.0 / held[1])[:1]
        out = out.T.astype(o_buf.dtype)
        o_buf[pl.ds(b * block_len, block_len), h] = out.reshape(block_len, share, head_dim)

    begin(0, 0)

    def several(step, first, t, sent):
        i = first + step * t
        for j in range(step):
            finish(i + j - 1)
            begin(i + j + 1, (j + 1) % BUFFERS)
            end(i + j, j % BUFFERS)
        done = lax.div(items[0, i + step - 1], heads)

        def ship(b, carry):
            shipped(b).start()
            return carry

        lax.fori_loop(sent, done, ship, 0)
        return done

    def shipped(b):
        rows = pl.ds(b * block_len, block_len)
        return pltpu.make_async_copy(o_buf.at[rows], o_hbm.at[rows], o_sem)

    many = lax.div(count, ITEMS)
    sent = lax.fori_loop(0, many, functools.partial(several, ITEMS, 0), 0)
    rest = count - many * ITEMS
    tail = pl.cdiv(rest, BUFFERS)
    sent = lax.fori_loop(0, tail, functools.partial(several, BUFFERS, many * ITEMS), sent)
    finish(many * ITEMS + BUFFERS * tail - 1)

    def ship_rest(b, carry):
        shipped(b).start()
        return carry

    lax.fori_loop(sent, blocks, ship_rest, 0)
    pltpu.make_async_copy(o_buf, o_hbm, o_sem).wait()


def on_device(queries, keys, values, chosen):
    tokens, query_heads, head_dim = queries.shape
    kv_heads, blocks, picks = chosen.shape
    block_len = tokens // blocks
    shards = lax.axis_size("ctx")
    heads = max(1, query_heads // (QUERY_HEADS // KEY_VALUE_HEADS))
    share = query_heads // heads
    width = block_len * share
    units = heads * blocks
    half = picks // 2
    partners = shards - 1
    held = units + partners * heads * 2
    vmem = pl.BlockSpec(memory_space=pltpu.VMEM)
    anywhere = pl.BlockSpec(memory_space=pltpu.HBM)
    q4 = jax.ShapeDtypeStruct((tokens, heads, share, head_dim), jnp.bfloat16)
    k_table = jax.ShapeDtypeStruct((held, block_len, 2 * head_dim), jnp.bfloat16)
    v_table = jax.ShapeDtypeStruct((held, head_dim, block_len), jnp.bfloat16)
    small = jax.ShapeDtypeStruct((units, 8, width), jnp.float32)
    large = jax.ShapeDtypeStruct((units, head_dim, width), jnp.float32)
    work = [
        pltpu.VMEM((BUFFERS, half * block_len, width), jnp.float32),
        pltpu.VMEM((BUFFERS, 8, width), jnp.float32),
    ]
    sent = (partners, 2, heads * 2, block_len, head_dim)
    q = queries.reshape(q4.shape)
    flat = (blocks, block_len * kv_heads, head_dim)
    plan, q, kt, vt, m, l, acc = pl.pallas_call(
        functools.partial(first_kernel, shards, query_heads),
        out_shape=[jax.ShapeDtypeStruct((heads * PLAN_ROWS, blocks), jnp.int32), q4, k_table, v_table, small, small, large],
        in_specs=[anywhere] * 4,
        out_specs=[vmem] * 7,
        scratch_shapes=[
            pltpu.VMEM((kv_heads, picks, blocks), jnp.int32),
            pltpu.VMEM((2, blocks, block_len * kv_heads, head_dim), jnp.bfloat16),
            pltpu.VMEM((heads * block_len, block_len * kv_heads), jnp.bfloat16),
            pltpu.VMEM((partners, 8, 128), jnp.int32),
            pltpu.VMEM((partners, 8, 128), jnp.int32),
            pltpu.SMEM((heads * PLAN_ROWS, blocks), jnp.int32),
            pltpu.VMEM(sent, jnp.bfloat16),
            pltpu.VMEM(sent, jnp.bfloat16),
            *work,
            pltpu.SemaphoreType.DMA,
            pltpu.SemaphoreType.DMA((2,)),
            pltpu.SemaphoreType.DMA,
            pltpu.SemaphoreType.DMA((partners,)),
            pltpu.SemaphoreType.DMA((partners,)),
            pltpu.SemaphoreType.DMA,
            pltpu.SemaphoreType.DMA((partners,)),
            pltpu.SemaphoreType.DMA((partners,)),
        ],
        compiler_params=pltpu.CompilerParams(
            collective_id=0, has_side_effects=True, vmem_limit_bytes=14 * 1024 * 1024
        ),
    )(
        *(pltpu.with_memory_space_constraint(x, pltpu.HBM) for x in (jnp.transpose(chosen, (0, 2, 1)), keys.reshape(flat), values.reshape(flat), q)),
    )
    out = pl.pallas_call(
        functools.partial(second_kernel, picks),
        out_shape=q4,
        in_specs=[pl.BlockSpec(memory_space=pltpu.SMEM)] + [vmem] * 6,
        out_specs=anywhere,
        scratch_shapes=[
            pltpu.SMEM((3, 2 * units + BUFFERS + 2), jnp.int32),
            pltpu.VMEM((2, 8, width), jnp.float32),
            pltpu.VMEM((head_dim, width), jnp.float32),
            pltpu.VMEM(q4.shape, jnp.bfloat16),
            pltpu.SemaphoreType.DMA,
            *work,
        ],
        compiler_params=pltpu.CompilerParams(vmem_limit_bytes=10 * 1024 * 1024),
    )(plan, q, kt, vt, m, l, acc)
    return out.reshape(tokens, query_heads, head_dim)


def solution(mesh):
    placed = (
        P(("groups", "ctx"), ("heads", "rep"), None),
        P(("groups", "ctx"), "heads", None),
        P(("groups", "ctx"), "heads", None),
        P("heads", ("groups", "ctx"), None),
    )
    return jax.shard_map(
        on_device,
        mesh=mesh,
        in_specs=placed,
        out_specs=P(("groups", "ctx"), ("heads", "rep"), None),
        check_vma=False,
    )
```

```python
import functools
import math

import jax
import jax.numpy as jnp
from jax import lax
from jax.experimental import pallas as pl
from jax.experimental.pallas import tpu as pltpu
from jax.sharding import PartitionSpec as P

QUERY_HEADS = 32
KEY_VALUE_HEADS = 8
REMOTE_BLOCK_MAX = 2
NEGATIVE = -1e30
BIG = 1 << 30
PLAN_ROWS = 16
SPLIT = 4
ITEMS = 8
LATER_ITEMS = 16
BUFFERS = 2
MESH = pl.DeviceIdType.MESH


def scaled_pair(k, factor):
    k = k * factor
    high = k.astype(jnp.bfloat16)
    low = (k - high.astype(jnp.float32)).astype(jnp.bfloat16)
    return jnp.concatenate([high, low], axis=1)


def score(q, keys, opens, causal, kt_ref, s_ref, t_ref):
    block_len = kt_ref.shape[1]
    width = q.shape[0]
    qa = jnp.concatenate([q, q], axis=1)
    ka = jnp.concatenate([kt_ref[k] for k in keys], axis=0)
    scores = lax.dot_general(ka, qa, (((1,), (1,)), ((), ())), preferred_element_type=jnp.float32)
    top = None
    for i, is_open in enumerate(opens):
        part = scores[i * block_len : (i + 1) * block_len]
        if causal and i == 0:
            key = lax.broadcasted_iota(jnp.int32, part.shape, 0)
            query = lax.div(lax.broadcasted_iota(jnp.int32, part.shape, 1), width // block_len)
            part = jnp.where(key <= query, part, NEGATIVE)
        s_ref[i * block_len : (i + 1) * block_len, :] = part
        part = jnp.max(part.reshape(-1, 8, width), axis=0)
        part = jnp.where(is_open, part, NEGATIVE)
        top = part if top is None else jnp.maximum(top, part)
    t_ref[...] = jnp.broadcast_to(jnp.max(top, axis=0, keepdims=True), (8, width))


def weigh(top, opens, block_len, s_ref):
    weights = []
    width = s_ref.shape[1]
    for i, is_open in enumerate(opens):
        less = jnp.where(is_open, top, -NEGATIVE)
        w = jnp.exp2(s_ref[i * block_len : (i + 1) * block_len, :].reshape(-1, 8, width) - less)
        weights.append(w.reshape(block_len, width).astype(jnp.bfloat16))
    return jnp.concatenate(weights, axis=0)


def weighted(keys, vt_ref, weights):
    head_dim = vt_ref.shape[1]
    values = jnp.concatenate([vt_ref[k] for k in keys], axis=1)
    values = jnp.concatenate([values, jnp.ones((16, values.shape[1]), values.dtype)], axis=0)
    out = jnp.dot(values, weights, preferred_element_type=jnp.float32)
    return out[:head_dim], out[head_dim : head_dim + 8]


def first_kernel(shards, query_heads, chosen_hbm, k_hbm, v_hbm, q_hbm, *refs):
    (plan_ref, q_ref, kt_ref, vt_ref, m_ref, l_ref, acc_ref) = refs[:7]
    (chosen_ref, raw, pick, ask, asked, plan_s, send, land, s_buf, t_buf) = refs[7:17]
    (chosen_sem, load_sem, q_sem, ask_send, ask_recv, plan_sem, block_send, block_recv) = refs[17:]
    me = lax.axis_index("ctx")
    tokens, heads, share, head_dim = q_ref.shape
    kv_heads, picks, blocks = chosen_ref.shape
    chosen_load = pltpu.make_async_copy(chosen_hbm, chosen_ref, chosen_sem)
    chosen_load.start()
    block_len = tokens // blocks
    width = block_len * share
    units = heads * blocks
    first_head = lax.axis_index("rep") * query_heads // (QUERY_HEADS // KEY_VALUE_HEADS)
    factor = head_dim**-0.5 * math.log2(math.e)
    barrier = pltpu.get_barrier_semaphore()
    for d in range(1, shards):
        pl.semaphore_signal(barrier, inc=1, device_id={"ctx": lax.rem(me + d, shards)}, device_id_type=MESH)
    loads = [pltpu.make_async_copy(src, raw.at[i], load_sem.at[i]) for i, src in enumerate((k_hbm, v_hbm))]
    for load in loads:
        load.start()
    q_load = pltpu.make_async_copy(q_hbm, q_ref, q_sem)

    lane = lax.broadcasted_iota(jnp.int32, (8, 128), 1)
    tiles = [jnp.zeros((8, 128), jnp.int32) for _ in range(1, shards)]
    base = me * blocks
    slot_of = []
    chosen_load.wait()
    for h in range(heads):
        chosen = chosen_ref[first_head + h]
        local = (chosen >= base) & (chosen < base + blocks)
        slot = jnp.where(local, chosen - base + h * blocks, 0)
        for d in range(1, shards):
            start = (me - d) * blocks
            inside = (chosen >= start) & (chosen < start + blocks)
            first = jnp.min(jnp.where(inside, chosen, BIG), keepdims=True)
            later = inside & (chosen > first)
            second = jnp.min(jnp.where(later, chosen, BIG), keepdims=True)
            slot = jnp.where(inside, units + ((d - 1) * heads + h) * 2 + later.astype(jnp.int32), slot)
            for r, place in enumerate((first, second)):
                place = jnp.clip(place - start, 0, blocks - 1)
                tiles[d - 1] = jnp.where(lane == h * 2 + r, place, tiles[d - 1])
        slot_of.append((chosen, slot))
    for d in range(1, shards):
        ask[d - 1] = tiles[d - 1]
    pl.semaphore_wait(barrier, shards - 1)

    def request(d):
        return pltpu.make_async_remote_copy(
            src_ref=ask.at[d - 1],
            dst_ref=asked.at[d - 1],
            send_sem=ask_send.at[d - 1],
            recv_sem=ask_recv.at[d - 1],
            device_id={"ctx": lax.rem(me - d + shards, shards)},
            device_id_type=MESH,
        )

    def deliver(d):
        return pltpu.make_async_remote_copy(
            src_ref=send.at[d - 1],
            dst_ref=land.at[d - 1],
            send_sem=block_send.at[d - 1],
            recv_sem=block_recv.at[d - 1],
            device_id={"ctx": lax.rem(me + d, shards)},
            device_id_type=MESH,
        )

    for d in range(1, shards):

        @pl.when(me >= d)
        def _(d=d):
            request(d).start()

    q_load.start()
    for h, (chosen, slot) in enumerate(slot_of):
        rows = [chosen[k : k + 1, :] for k in range(picks)]
        slots = [slot[k : k + 1, :] for k in range(picks)]
        near = [(x >= base) & (x < base + blocks) for x in rows]
        is_local, is_remote = [], []
        for k in range(picks):
            fresh = jnp.ones(rows[k].shape, jnp.int32)
            for j in range(k):
                fresh = jnp.where(rows[j] == rows[k], 0, fresh)
            is_local.append(jnp.where(near[k], fresh, 0))
            is_remote.append(jnp.where(near[k], 0, fresh))
        local_count = functools.reduce(jnp.add, is_local)
        place_of, at_local, at_remote = [], jnp.zeros_like(local_count), local_count
        for k in range(picks):
            place = jnp.where(is_local[k] > 0, at_local, at_remote)
            place_of.append(jnp.where(is_local[k] + is_remote[k] > 0, place, picks))
            at_local = at_local + is_local[k]
            at_remote = at_remote + is_remote[k]
        for p in range(picks):
            total = jnp.zeros_like(local_count)
            for k in range(picks):
                total = jnp.where(place_of[k] == p, slots[k], total)
            plan_ref[h * PLAN_ROWS + p : h * PLAN_ROWS + p + 1, :] = total
        plan_ref[h * PLAN_ROWS + picks : h * PLAN_ROWS + picks + 1, :] = local_count
        plan_ref[h * PLAN_ROWS + picks + 1 : h * PLAN_ROWS + picks + 2, :] = at_remote
        for p in range(picks + 2, PLAN_ROWS):
            plan_ref[h * PLAN_ROWS + p : h * PLAN_ROWS + p + 1, :] = jnp.zeros_like(local_count)
    plan_copy = pltpu.make_async_copy(plan_ref, plan_s, plan_sem)
    plan_copy.start()
    for load in loads:
        load.wait()
    wide = kv_heads * block_len
    out_row = lax.broadcasted_iota(jnp.int32, (heads * block_len, wide), 0)
    in_row = lax.broadcasted_iota(jnp.int32, (heads * block_len, wide), 1)
    source = lax.rem(out_row, block_len) * kv_heads + first_head + lax.div(out_row, block_len)
    pick[...] = jnp.where(source == in_row, 1.0, 0.0).astype(jnp.bfloat16)

    def parted(b, rows):
        both = jnp.concatenate([raw[0, b], raw[1, b]], axis=1)
        both = jnp.dot(pick[rows, :], both, preferred_element_type=jnp.float32)
        return both[:, :head_dim], both[:, head_dim:]

    for d in range(shards - 1, 0, -1):

        @pl.when(me + d < shards)
        def _(d=d):
            request(d).wait_recv()
            places = asked[d - 1]
            for h in range(heads):
                for r in range(2):
                    place = jnp.max(jnp.where(lane == h * 2 + r, places, 0))
                    k, v = parted(place, slice(h * block_len, (h + 1) * block_len))
                    send[d - 1, 0, h * 2 + r] = k.astype(jnp.bfloat16)
                    send[d - 1, 1, h * 2 + r] = v.T.astype(jnp.bfloat16)
            deliver(d).start()

    def split(t, carry):
        for j in range(SPLIT):
            b = jnp.minimum(t * SPLIT + j, blocks - 1)
            k, v = parted(b, slice(0, heads * block_len))
            for h in range(heads):
                rows = slice(h * block_len, (h + 1) * block_len)
                kt_ref[h * blocks + b] = scaled_pair(k[rows, :], factor)
                vt_ref[h * blocks + b] = v[rows, :].T.astype(jnp.bfloat16)
        return carry

    lax.fori_loop(0, pl.cdiv(blocks, SPLIT), split, 0)
    plan_copy.wait()
    q_load.wait()
    half = picks // 2

    def slots_of(u):
        h, b = lax.rem(u, heads), lax.div(u, heads)
        near = plan_s[h * PLAN_ROWS + picks, b]
        keys = [jnp.where(p < near, plan_s[h * PLAN_ROWS + p, b], 0) for p in range(half)]
        return h, b, keys, [p < near for p in range(half)]

    def begin(u, buf):
        h, b, keys, opens = slots_of(u)
        q = q_ref[pl.ds(b * block_len, block_len), h].reshape(width, head_dim)
        score(q, keys, opens, True, kt_ref, s_buf.at[buf], t_buf.at[buf])

    def end(u, buf):
        h, b, keys, opens = slots_of(u)
        top = t_buf[buf]
        weights = weigh(top, opens, block_len, s_buf.at[buf])
        m_ref[u] = top
        acc_ref[u], l_ref[u] = weighted(keys, vt_ref, weights)

    begin(0, 0)

    def several(t, carry):
        u = ITEMS * t
        for j in range(ITEMS):
            begin(jnp.minimum(u + j + 1, units - 1), (j + 1) % BUFFERS)
            end(jnp.minimum(u + j, units - 1), j % BUFFERS)
        return carry

    lax.fori_loop(0, pl.cdiv(units, ITEMS), several, 0)

    for d in range(1, shards):

        @pl.when(me >= d)
        def _(d=d):
            deliver(d).wait_recv()
            at = units + (d - 1) * heads * 2
            for j in range(heads * 2):
                kt_ref[at + j] = scaled_pair(land[d - 1, 0, j].astype(jnp.float32), factor)
                vt_ref[at + j] = land[d - 1, 1, j]

    for d in range(1, shards):

        @pl.when(me >= d)
        def _(d=d):
            request(d).wait_send()

        @pl.when(me + d < shards)
        def _(d=d):
            deliver(d).wait_send()


def second_kernel(picks, plan, q_ref, kt_ref, vt_ref, m_ref, l_ref, acc_ref, o_hbm, items, held, held_acc, o_buf, o_sem, *work):
    s_buf, t_buf = work
    tokens, heads, share, head_dim = q_ref.shape
    units = acc_ref.shape[0]
    blocks = units // heads
    block_len = tokens // blocks
    width = block_len * share
    half = picks // 2

    def lay(b, count):
        for h in range(heads):
            at = jnp.minimum(plan[h * PLAN_ROWS + picks, b], half)
            more = plan[h * PLAN_ROWS + picks + 1, b] - at > half
            for j in range(2):
                items[0, count + j] = b * heads + h
                items[1, count + j] = at + j * half
                items[2, count + j] = j
            count = count + 1 + more.astype(jnp.int32)
        return count

    count = lax.fori_loop(0, blocks, lay, 0, unroll=4)
    for i in range(BUFFERS + 1):
        items[0, count + i] = units - 1
        items[1, count + i] = picks
        items[2, count + i] = 1

    def slots_of(i):
        u, at = items[0, i], items[1, i]
        h, b = lax.rem(u, heads), lax.div(u, heads)
        every = plan[h * PLAN_ROWS + picks + 1, b]
        inside = [at + p < every for p in range(half)]
        keys = [jnp.where(x, plan[h * PLAN_ROWS + jnp.minimum(at + p, picks - 1), b], 0) for p, x in enumerate(inside)]
        return u, h, b, keys, inside

    def begin(i, buf):
        u, h, b, keys, opens = slots_of(i)
        q = q_ref[pl.ds(b * block_len, block_len), h].reshape(width, head_dim)
        score(q, keys, opens, False, kt_ref, s_buf.at[buf], t_buf.at[buf])

    def end(i, buf):
        u, h, b, keys, opens = slots_of(i)
        again = items[2, i] > 0
        old = jnp.where(again, held[0], m_ref[u])
        top = jnp.maximum(old, t_buf[buf])
        keep = jnp.exp2(old - top)
        weights = weigh(top, opens, block_len, s_buf.at[buf])
        out, total = weighted(keys, vt_ref, weights)
        total = jnp.where(again, held[1], l_ref[u]) * keep + total
        out = jnp.where(again, held_acc[...], acc_ref[u]) * keep[:1] + out
        held[0] = top
        held[1] = total
        held_acc[...] = out

    def finish(i):
        u = items[0, jnp.maximum(i, 0)]
        h, b = lax.rem(u, heads), lax.div(u, heads)
        out = held_acc[...] * (1.0 / held[1])[:1]
        out = out.T.astype(o_buf.dtype)
        o_buf[pl.ds(b * block_len, block_len), h] = out.reshape(block_len, share, head_dim)

    begin(0, 0)

    def several(step, first, t, sent):
        i = first + step * t
        for j in range(step):
            finish(i + j - 1)
            begin(i + j + 1, (j + 1) % BUFFERS)
            end(i + j, j % BUFFERS)
        done = lax.div(items[0, i + step - 1], heads)

        def ship(b, carry):
            shipped(b).start()
            return carry

        lax.fori_loop(sent, done, ship, 0)
        return done

    def shipped(b):
        rows = pl.ds(b * block_len, block_len)
        return pltpu.make_async_copy(o_buf.at[rows], o_hbm.at[rows], o_sem)

    many = lax.div(count, LATER_ITEMS)
    sent = lax.fori_loop(0, many, functools.partial(several, LATER_ITEMS, 0), 0)
    rest = count - many * LATER_ITEMS
    tail = pl.cdiv(rest, BUFFERS)
    sent = lax.fori_loop(0, tail, functools.partial(several, BUFFERS, many * LATER_ITEMS), sent)
    finish(many * LATER_ITEMS + BUFFERS * tail - 1)

    def ship_rest(b, carry):
        shipped(b).start()
        return carry

    lax.fori_loop(sent, blocks, ship_rest, 0)
    pltpu.make_async_copy(o_buf, o_hbm, o_sem).wait()


def on_device(queries, keys, values, chosen):
    tokens, query_heads, head_dim = queries.shape
    kv_heads, blocks, picks = chosen.shape
    block_len = tokens // blocks
    shards = lax.axis_size("ctx")
    heads = max(1, query_heads // (QUERY_HEADS // KEY_VALUE_HEADS))
    share = query_heads // heads
    width = block_len * share
    units = heads * blocks
    half = picks // 2
    partners = shards - 1
    held = units + partners * heads * 2
    vmem = pl.BlockSpec(memory_space=pltpu.VMEM)
    anywhere = pl.BlockSpec(memory_space=pltpu.HBM)
    q4 = jax.ShapeDtypeStruct((tokens, heads, share, head_dim), jnp.bfloat16)
    k_table = jax.ShapeDtypeStruct((held, block_len, 2 * head_dim), jnp.bfloat16)
    v_table = jax.ShapeDtypeStruct((held, head_dim, block_len), jnp.bfloat16)
    small = jax.ShapeDtypeStruct((units, 8, width), jnp.float32)
    large = jax.ShapeDtypeStruct((units, head_dim, width), jnp.float32)
    work = [
        pltpu.VMEM((BUFFERS, half * block_len, width), jnp.float32),
        pltpu.VMEM((BUFFERS, 8, width), jnp.float32),
    ]
    sent = (partners, 2, heads * 2, block_len, head_dim)
    q = queries.reshape(q4.shape)
    flat = (blocks, block_len * kv_heads, head_dim)
    plan, q, kt, vt, m, l, acc = pl.pallas_call(
        functools.partial(first_kernel, shards, query_heads),
        out_shape=[jax.ShapeDtypeStruct((heads * PLAN_ROWS, blocks), jnp.int32), q4, k_table, v_table, small, small, large],
        in_specs=[anywhere] * 4,
        out_specs=[vmem] * 7,
        scratch_shapes=[
            pltpu.VMEM((kv_heads, picks, blocks), jnp.int32),
            pltpu.VMEM((2, blocks, block_len * kv_heads, head_dim), jnp.bfloat16),
            pltpu.VMEM((heads * block_len, block_len * kv_heads), jnp.bfloat16),
            pltpu.VMEM((partners, 8, 128), jnp.int32),
            pltpu.VMEM((partners, 8, 128), jnp.int32),
            pltpu.SMEM((heads * PLAN_ROWS, blocks), jnp.int32),
            pltpu.VMEM(sent, jnp.bfloat16),
            pltpu.VMEM(sent, jnp.bfloat16),
            *work,
            pltpu.SemaphoreType.DMA,
            pltpu.SemaphoreType.DMA((2,)),
            pltpu.SemaphoreType.DMA,
            pltpu.SemaphoreType.DMA((partners,)),
            pltpu.SemaphoreType.DMA((partners,)),
            pltpu.SemaphoreType.DMA,
            pltpu.SemaphoreType.DMA((partners,)),
            pltpu.SemaphoreType.DMA((partners,)),
        ],
        compiler_params=pltpu.CompilerParams(
            collective_id=0, has_side_effects=True, vmem_limit_bytes=14 * 1024 * 1024
        ),
    )(
        *(pltpu.with_memory_space_constraint(x, pltpu.HBM) for x in (jnp.transpose(chosen, (0, 2, 1)), keys.reshape(flat), values.reshape(flat), q)),
    )
    out = pl.pallas_call(
        functools.partial(second_kernel, picks),
        out_shape=q4,
        in_specs=[pl.BlockSpec(memory_space=pltpu.SMEM)] + [vmem] * 6,
        out_specs=anywhere,
        scratch_shapes=[
            pltpu.SMEM((3, 2 * units + BUFFERS + 2), jnp.int32),
            pltpu.VMEM((2, 8, width), jnp.float32),
            pltpu.VMEM((head_dim, width), jnp.float32),
            pltpu.VMEM(q4.shape, jnp.bfloat16),
            pltpu.SemaphoreType.DMA,
            *work,
        ],
        compiler_params=pltpu.CompilerParams(vmem_limit_bytes=10 * 1024 * 1024),
    )(plan, q, kt, vt, m, l, acc)
    return out.reshape(tokens, query_heads, head_dim)


def solution(mesh):
    placed = (
        P(("groups", "ctx"), ("heads", "rep"), None),
        P(("groups", "ctx"), "heads", None),
        P(("groups", "ctx"), "heads", None),
        P("heads", ("groups", "ctx"), None),
    )
    return jax.shard_map(
        on_device,
        mesh=mesh,
        in_specs=placed,
        out_specs=P(("groups", "ctx"), ("heads", "rep"), None),
        check_vma=False,
    )
```

```python
import functools
import math

import jax
import jax.numpy as jnp
from jax import lax
from jax.experimental import pallas as pl
from jax.experimental.pallas import tpu as pltpu
from jax.sharding import PartitionSpec as P

QUERY_HEADS = 32
KEY_VALUE_HEADS = 8
REMOTE_BLOCK_MAX = 2
NEGATIVE = -1e30
BIG = 1 << 30
PLAN_ROWS = 16
SPLIT = 4
ITEMS = 8
LATER_ITEMS = 16
BUFFERS = 2
MESH = pl.DeviceIdType.MESH


def scaled_pair(k, factor):
    k = k * factor
    high = k.astype(jnp.bfloat16)
    low = (k - high.astype(jnp.float32)).astype(jnp.bfloat16)
    return jnp.concatenate([high, low], axis=1)


def score(q, keys, opens, causal, kt_ref, s_ref, t_ref):
    block_len = kt_ref.shape[1]
    width = q.shape[0]
    qa = jnp.concatenate([q, q], axis=1)
    ka = jnp.concatenate([kt_ref[k] for k in keys], axis=0)
    scores = lax.dot_general(ka, qa, (((1,), (1,)), ((), ())), preferred_element_type=jnp.float32)
    top = None
    for i, is_open in enumerate(opens):
        part = scores[i * block_len : (i + 1) * block_len]
        if causal and i == 0:
            key = lax.broadcasted_iota(jnp.int32, part.shape, 0)
            query = lax.div(lax.broadcasted_iota(jnp.int32, part.shape, 1), width // block_len)
            part = jnp.where(key <= query, part, NEGATIVE)
        s_ref[i * block_len : (i + 1) * block_len, :] = part
        part = jnp.max(part.reshape(-1, 8, width), axis=0)
        part = jnp.where(is_open, part, NEGATIVE)
        top = part if top is None else jnp.maximum(top, part)
    t_ref[...] = jnp.broadcast_to(jnp.max(top, axis=0, keepdims=True), (8, width))


def weigh(top, opens, block_len, s_ref):
    weights = []
    width = s_ref.shape[1]
    for i, is_open in enumerate(opens):
        less = jnp.where(is_open, top, -NEGATIVE)
        w = jnp.exp2(s_ref[i * block_len : (i + 1) * block_len, :].reshape(-1, 8, width) - less)
        weights.append(w.reshape(block_len, width).astype(jnp.bfloat16))
    return jnp.concatenate(weights, axis=0)


def weighted(keys, vt_ref, weights):
    head_dim = vt_ref.shape[1]
    values = jnp.concatenate([vt_ref[k] for k in keys], axis=1)
    values = jnp.concatenate([values, jnp.ones((8, values.shape[1]), values.dtype)], axis=0)
    out = jnp.dot(values, weights, preferred_element_type=jnp.float32)
    return out[:head_dim], out[head_dim : head_dim + 8]


def first_kernel(shards, query_heads, chosen_hbm, k_hbm, v_hbm, q_hbm, *refs):
    (plan_ref, q_ref, kt_ref, vt_ref, m_ref, l_ref, acc_ref) = refs[:7]
    (chosen_ref, raw, pick, ask, asked, plan_s, send, land, s_buf, t_buf) = refs[7:17]
    (chosen_sem, load_sem, q_sem, ask_send, ask_recv, plan_sem, block_send, block_recv) = refs[17:]
    me = lax.axis_index("ctx")
    tokens, heads, share, head_dim = q_ref.shape
    kv_heads, picks, blocks = chosen_ref.shape
    chosen_load = pltpu.make_async_copy(chosen_hbm, chosen_ref, chosen_sem)
    chosen_load.start()
    block_len = tokens // blocks
    width = block_len * share
    units = heads * blocks
    first_head = lax.axis_index("rep") * query_heads // (QUERY_HEADS // KEY_VALUE_HEADS)
    factor = head_dim**-0.5 * math.log2(math.e)
    barrier = pltpu.get_barrier_semaphore()
    for d in range(1, shards):
        pl.semaphore_signal(barrier, inc=1, device_id={"ctx": lax.rem(me + d, shards)}, device_id_type=MESH)
    loads = [pltpu.make_async_copy(src, raw.at[i], load_sem.at[i]) for i, src in enumerate((k_hbm, v_hbm))]
    for load in loads:
        load.start()
    q_load = pltpu.make_async_copy(q_hbm, q_ref, q_sem)

    lane = lax.broadcasted_iota(jnp.int32, (8, 128), 1)
    tiles = [jnp.zeros((8, 128), jnp.int32) for _ in range(1, shards)]
    base = me * blocks
    slot_of = []
    chosen_load.wait()
    for h in range(heads):
        chosen = chosen_ref[first_head + h]
        local = (chosen >= base) & (chosen < base + blocks)
        slot = jnp.where(local, chosen - base + h * blocks, 0)
        for d in range(1, shards):
            start = (me - d) * blocks
            inside = (chosen >= start) & (chosen < start + blocks)
            first = jnp.min(jnp.where(inside, chosen, BIG), keepdims=True)
            later = inside & (chosen > first)
            second = jnp.min(jnp.where(later, chosen, BIG), keepdims=True)
            slot = jnp.where(inside, units + ((d - 1) * heads + h) * 2 + later.astype(jnp.int32), slot)
            for r, place in enumerate((first, second)):
                place = jnp.clip(place - start, 0, blocks - 1)
                tiles[d - 1] = jnp.where(lane == h * 2 + r, place, tiles[d - 1])
        slot_of.append((chosen, slot))
    for d in range(1, shards):
        ask[d - 1] = tiles[d - 1]
    pl.semaphore_wait(barrier, shards - 1)

    def request(d):
        return pltpu.make_async_remote_copy(
            src_ref=ask.at[d - 1],
            dst_ref=asked.at[d - 1],
            send_sem=ask_send.at[d - 1],
            recv_sem=ask_recv.at[d - 1],
            device_id={"ctx": lax.rem(me - d + shards, shards)},
            device_id_type=MESH,
        )

    def deliver(d):
        return pltpu.make_async_remote_copy(
            src_ref=send.at[d - 1],
            dst_ref=land.at[d - 1],
            send_sem=block_send.at[d - 1],
            recv_sem=block_recv.at[d - 1],
            device_id={"ctx": lax.rem(me + d, shards)},
            device_id_type=MESH,
        )

    for d in range(1, shards):

        @pl.when(me >= d)
        def _(d=d):
            request(d).start()

    q_load.start()
    for h, (chosen, slot) in enumerate(slot_of):
        rows = [chosen[k : k + 1, :] for k in range(picks)]
        slots = [slot[k : k + 1, :] for k in range(picks)]
        near = [(x >= base) & (x < base + blocks) for x in rows]
        is_local, is_remote = [], []
        for k in range(picks):
            fresh = jnp.ones(rows[k].shape, jnp.int32)
            for j in range(k):
                fresh = jnp.where(rows[j] == rows[k], 0, fresh)
            is_local.append(jnp.where(near[k], fresh, 0))
            is_remote.append(jnp.where(near[k], 0, fresh))
        local_count = functools.reduce(jnp.add, is_local)
        place_of, at_local, at_remote = [], jnp.zeros_like(local_count), local_count
        for k in range(picks):
            place = jnp.where(is_local[k] > 0, at_local, at_remote)
            place_of.append(jnp.where(is_local[k] + is_remote[k] > 0, place, picks))
            at_local = at_local + is_local[k]
            at_remote = at_remote + is_remote[k]
        for p in range(picks):
            total = jnp.zeros_like(local_count)
            for k in range(picks):
                total = jnp.where(place_of[k] == p, slots[k], total)
            plan_ref[h * PLAN_ROWS + p : h * PLAN_ROWS + p + 1, :] = total
        plan_ref[h * PLAN_ROWS + picks : h * PLAN_ROWS + picks + 1, :] = local_count
        plan_ref[h * PLAN_ROWS + picks + 1 : h * PLAN_ROWS + picks + 2, :] = at_remote
        for p in range(picks + 2, PLAN_ROWS):
            plan_ref[h * PLAN_ROWS + p : h * PLAN_ROWS + p + 1, :] = jnp.zeros_like(local_count)
    plan_copy = pltpu.make_async_copy(plan_ref, plan_s, plan_sem)
    plan_copy.start()
    for load in loads:
        load.wait()
    wide = kv_heads * block_len
    out_row = lax.broadcasted_iota(jnp.int32, (heads * block_len, wide), 0)
    in_row = lax.broadcasted_iota(jnp.int32, (heads * block_len, wide), 1)
    source = lax.rem(out_row, block_len) * kv_heads + first_head + lax.div(out_row, block_len)
    pick[...] = jnp.where(source == in_row, 1.0, 0.0).astype(jnp.bfloat16)

    def parted(b, rows):
        both = jnp.concatenate([raw[0, b], raw[1, b]], axis=1)
        both = jnp.dot(pick[rows, :], both, preferred_element_type=jnp.float32)
        return both[:, :head_dim], both[:, head_dim:]

    for d in range(shards - 1, 0, -1):

        @pl.when(me + d < shards)
        def _(d=d):
            request(d).wait_recv()
            places = asked[d - 1]
            for h in range(heads):
                for r in range(2):
                    place = jnp.max(jnp.where(lane == h * 2 + r, places, 0))
                    k, v = parted(place, slice(h * block_len, (h + 1) * block_len))
                    send[d - 1, 0, h * 2 + r] = k.astype(jnp.bfloat16)
                    send[d - 1, 1, h * 2 + r] = v.T.astype(jnp.bfloat16)
            deliver(d).start()

    def split(t, carry):
        for j in range(SPLIT):
            b = jnp.minimum(t * SPLIT + j, blocks - 1)
            k, v = parted(b, slice(0, heads * block_len))
            for h in range(heads):
                rows = slice(h * block_len, (h + 1) * block_len)
                kt_ref[h * blocks + b] = scaled_pair(k[rows, :], factor)
                vt_ref[h * blocks + b] = v[rows, :].T.astype(jnp.bfloat16)
        return carry

    lax.fori_loop(0, pl.cdiv(blocks, SPLIT), split, 0)
    plan_copy.wait()
    q_load.wait()
    half = picks // 2

    def slots_of(u):
        h, b = lax.rem(u, heads), lax.div(u, heads)
        near = plan_s[h * PLAN_ROWS + picks, b]
        keys = [jnp.where(p < near, plan_s[h * PLAN_ROWS + p, b], 0) for p in range(half)]
        return h, b, keys, [p < near for p in range(half)]

    def begin(u, buf):
        h, b, keys, opens = slots_of(u)
        q = q_ref[pl.ds(b * block_len, block_len), h].reshape(width, head_dim)
        score(q, keys, opens, True, kt_ref, s_buf.at[buf], t_buf.at[buf])

    def end(u, buf):
        h, b, keys, opens = slots_of(u)
        top = t_buf[buf]
        weights = weigh(top, opens, block_len, s_buf.at[buf])
        m_ref[u] = top
        acc_ref[u], l_ref[u] = weighted(keys, vt_ref, weights)

    begin(0, 0)

    def several(t, carry):
        u = ITEMS * t
        for j in range(ITEMS):
            begin(jnp.minimum(u + j + 1, units - 1), (j + 1) % BUFFERS)
            end(jnp.minimum(u + j, units - 1), j % BUFFERS)
        return carry

    lax.fori_loop(0, pl.cdiv(units, ITEMS), several, 0)

    for d in range(1, shards):

        @pl.when(me >= d)
        def _(d=d):
            deliver(d).wait_recv()
            at = units + (d - 1) * heads * 2
            for j in range(heads * 2):
                kt_ref[at + j] = scaled_pair(land[d - 1, 0, j].astype(jnp.float32), factor)
                vt_ref[at + j] = land[d - 1, 1, j]

    for d in range(1, shards):

        @pl.when(me >= d)
        def _(d=d):
            request(d).wait_send()

        @pl.when(me + d < shards)
        def _(d=d):
            deliver(d).wait_send()


def second_kernel(picks, plan, q_ref, kt_ref, vt_ref, m_ref, l_ref, acc_ref, o_hbm, items, held, held_acc, o_buf, o_sem, *work):
    s_buf, t_buf = work
    tokens, heads, share, head_dim = q_ref.shape
    units = acc_ref.shape[0]
    blocks = units // heads
    block_len = tokens // blocks
    width = block_len * share
    half = picks // 2

    def lay(b, count):
        for h in range(heads):
            at = jnp.minimum(plan[h * PLAN_ROWS + picks, b], half)
            more = plan[h * PLAN_ROWS + picks + 1, b] - at > half
            for j in range(2):
                items[0, count + j] = b * heads + h
                items[1, count + j] = at + j * half
                items[2, count + j] = j
            count = count + 1 + more.astype(jnp.int32)
        return count

    count = lax.fori_loop(0, blocks, lay, 0, unroll=4)
    for i in range(BUFFERS + 1):
        items[0, count + i] = units - 1
        items[1, count + i] = picks
        items[2, count + i] = 1

    def slots_of(i):
        u, at = items[0, i], items[1, i]
        h, b = lax.rem(u, heads), lax.div(u, heads)
        every = plan[h * PLAN_ROWS + picks + 1, b]
        inside = [at + p < every for p in range(half)]
        keys = [jnp.where(x, plan[h * PLAN_ROWS + jnp.minimum(at + p, picks - 1), b], 0) for p, x in enumerate(inside)]
        return u, h, b, keys, inside

    def begin(i, buf):
        u, h, b, keys, opens = slots_of(i)
        q = q_ref[pl.ds(b * block_len, block_len), h].reshape(width, head_dim)
        score(q, keys, opens, False, kt_ref, s_buf.at[buf], t_buf.at[buf])

    def end(i, buf):
        u, h, b, keys, opens = slots_of(i)
        again = items[2, i] > 0
        old = jnp.where(again, held[0], m_ref[u])
        top = jnp.maximum(old, t_buf[buf])
        keep = jnp.exp2(old - top)
        weights = weigh(top, opens, block_len, s_buf.at[buf])
        out, total = weighted(keys, vt_ref, weights)
        total = jnp.where(again, held[1], l_ref[u]) * keep + total
        out = jnp.where(again, held_acc[...], acc_ref[u]) * keep[:1] + out
        held[0] = top
        held[1] = total
        held_acc[...] = out

    def finish(i):
        u = items[0, jnp.maximum(i, 0)]
        h, b = lax.rem(u, heads), lax.div(u, heads)
        out = held_acc[...] * (1.0 / held[1])[:1]
        out = out.T.astype(o_buf.dtype)
        o_buf[pl.ds(b * block_len, block_len), h] = out.reshape(block_len, share, head_dim)

    begin(0, 0)

    def several(step, first, t, sent):
        i = first + step * t
        for j in range(step):
            finish(i + j - 1)
            begin(i + j + 1, (j + 1) % BUFFERS)
            end(i + j, j % BUFFERS)
        done = lax.div(items[0, i + step - 1], heads)

        def ship(b, carry):
            shipped(b).start()
            return carry

        lax.fori_loop(sent, done, ship, 0)
        return done

    def shipped(b):
        rows = pl.ds(b * block_len, block_len)
        return pltpu.make_async_copy(o_buf.at[rows], o_hbm.at[rows], o_sem)

    many = lax.div(count, LATER_ITEMS)
    sent = lax.fori_loop(0, many, functools.partial(several, LATER_ITEMS, 0), 0)
    rest = count - many * LATER_ITEMS
    tail = pl.cdiv(rest, BUFFERS)
    sent = lax.fori_loop(0, tail, functools.partial(several, BUFFERS, many * LATER_ITEMS), sent)
    finish(many * LATER_ITEMS + BUFFERS * tail - 1)

    def ship_rest(b, carry):
        shipped(b).start()
        return carry

    lax.fori_loop(sent, blocks, ship_rest, 0)
    pltpu.make_async_copy(o_buf, o_hbm, o_sem).wait()


def on_device(queries, keys, values, chosen):
    tokens, query_heads, head_dim = queries.shape
    kv_heads, blocks, picks = chosen.shape
    block_len = tokens // blocks
    shards = lax.axis_size("ctx")
    heads = max(1, query_heads // (QUERY_HEADS // KEY_VALUE_HEADS))
    share = query_heads // heads
    width = block_len * share
    units = heads * blocks
    half = picks // 2
    partners = shards - 1
    held = units + partners * heads * 2
    vmem = pl.BlockSpec(memory_space=pltpu.VMEM)
    anywhere = pl.BlockSpec(memory_space=pltpu.HBM)
    q4 = jax.ShapeDtypeStruct((tokens, heads, share, head_dim), jnp.bfloat16)
    k_table = jax.ShapeDtypeStruct((held, block_len, 2 * head_dim), jnp.bfloat16)
    v_table = jax.ShapeDtypeStruct((held, head_dim, block_len), jnp.bfloat16)
    small = jax.ShapeDtypeStruct((units, 8, width), jnp.float32)
    large = jax.ShapeDtypeStruct((units, head_dim, width), jnp.float32)
    work = [
        pltpu.VMEM((BUFFERS, half * block_len, width), jnp.float32),
        pltpu.VMEM((BUFFERS, 8, width), jnp.float32),
    ]
    sent = (partners, 2, heads * 2, block_len, head_dim)
    q = queries.reshape(q4.shape)
    flat = (blocks, block_len * kv_heads, head_dim)
    plan, q, kt, vt, m, l, acc = pl.pallas_call(
        functools.partial(first_kernel, shards, query_heads),
        out_shape=[jax.ShapeDtypeStruct((heads * PLAN_ROWS, blocks), jnp.int32), q4, k_table, v_table, small, small, large],
        in_specs=[anywhere] * 4,
        out_specs=[vmem] * 7,
        scratch_shapes=[
            pltpu.VMEM((kv_heads, picks, blocks), jnp.int32),
            pltpu.VMEM((2, blocks, block_len * kv_heads, head_dim), jnp.bfloat16),
            pltpu.VMEM((heads * block_len, block_len * kv_heads), jnp.bfloat16),
            pltpu.VMEM((partners, 8, 128), jnp.int32),
            pltpu.VMEM((partners, 8, 128), jnp.int32),
            pltpu.SMEM((heads * PLAN_ROWS, blocks), jnp.int32),
            pltpu.VMEM(sent, jnp.bfloat16),
            pltpu.VMEM(sent, jnp.bfloat16),
            *work,
            pltpu.SemaphoreType.DMA,
            pltpu.SemaphoreType.DMA((2,)),
            pltpu.SemaphoreType.DMA,
            pltpu.SemaphoreType.DMA((partners,)),
            pltpu.SemaphoreType.DMA((partners,)),
            pltpu.SemaphoreType.DMA,
            pltpu.SemaphoreType.DMA((partners,)),
            pltpu.SemaphoreType.DMA((partners,)),
        ],
        compiler_params=pltpu.CompilerParams(
            collective_id=0, has_side_effects=True, vmem_limit_bytes=14 * 1024 * 1024
        ),
    )(
        *(pltpu.with_memory_space_constraint(x, pltpu.HBM) for x in (jnp.transpose(chosen, (0, 2, 1)), keys.reshape(flat), values.reshape(flat), q)),
    )
    out = pl.pallas_call(
        functools.partial(second_kernel, picks),
        out_shape=q4,
        in_specs=[pl.BlockSpec(memory_space=pltpu.SMEM)] + [vmem] * 6,
        out_specs=anywhere,
        scratch_shapes=[
            pltpu.SMEM((3, 2 * units + BUFFERS + 2), jnp.int32),
            pltpu.VMEM((2, 8, width), jnp.float32),
            pltpu.VMEM((head_dim, width), jnp.float32),
            pltpu.VMEM(q4.shape, jnp.bfloat16),
            pltpu.SemaphoreType.DMA,
            *work,
        ],
        compiler_params=pltpu.CompilerParams(vmem_limit_bytes=10 * 1024 * 1024),
    )(plan, q, kt, vt, m, l, acc)
    return out.reshape(tokens, query_heads, head_dim)


def solution(mesh):
    placed = (
        P(("groups", "ctx"), ("heads", "rep"), None),
        P(("groups", "ctx"), "heads", None),
        P(("groups", "ctx"), "heads", None),
        P("heads", ("groups", "ctx"), None),
    )
    return jax.shard_map(
        on_device,
        mesh=mesh,
        in_specs=placed,
        out_specs=P(("groups", "ctx"), ("heads", "rep"), None),
        check_vma=False,
    )
```
